512 devices in a mesh: expert: 64 (over y, x, core), fsdp: 8 (over z).
Axes of the slice: x: 4, y: 8, z: 8, core: 2. Of those that a mesh axis runs over, the one named last changes fastest.
Arguments:
- tokens: bfloat16 [1024, 6144], P('expert', 'fsdp'), may hold values from -6 to 6
- expert_ids: int32 [1024, 2], P('expert'), may hold values from 0 to 3, all different within a row; in each aligned block of 16 rows (0 to 15, 16 to 31, ...) at most 10 rows name the same one
- route_logits: float32 [1024, 2], P('expert'), may hold values from -6 to 6
- w_gate: bfloat16 [6144, 32768], P('fsdp', 'expert'), may hold values from -0.078125 to 0.078125
- w_up: bfloat16 [6144, 32768], P('fsdp', 'expert'), may hold values from -0.078125 to 0.078125
- w_down: bfloat16 [32768, 6144], P('expert', 'fsdp'), may hold values from -0.0625 to 0.0625
- out_grad: bfloat16 [1024, 6144], P('expert', 'fsdp'), may hold values from -6 to 6
Outputs:
- layer_out: bfloat16 [1024, 6144], P('expert', 'fsdp')
- tokens_grad: bfloat16 [1024, 6144], P('expert', 'fsdp')
- gate_grad: bfloat16 [6144, 32768], P('fsdp', 'expert')
- up_grad: bfloat16 [6144, 32768], P('fsdp', 'expert')
- down_grad: bfloat16 [32768, 6144], P('expert', 'fsdp')
- logits_grad: float32 [1024, 2], P('expert')
The draws below stay inside these ranges and needn't reach their ends.
Inputs may be any that keep to these rules, and one draw needn't show every extreme that they name: `expert_ids`: each token names 2 different experts; among the 16 tokens of one index of the expert axis no expert is named by more than 10 tokens, a bound that some block reaches.
All inputs are finite; a program needn't handle non-finite values.
Results may differ from the reference program's by a relative error of at most 0.033.
Values may be sent and summed in bfloat16 or wider, within the bound.
No kernel may reach another device: no remote copies, remote signals or barrier semaphores. Data moves between devices by JAX's collectives and lax.ppermute only.
A program may use at most 64 MiB of HBM per device.

```python
import math
import jax
import jax.numpy as jnp
import numpy as np
from jax import lax

D = 6144
FF = 8192
EXPERTS = 4
TOP = 2
TOK_DEV = 16
MOST = 10
TOKENS = 1024
N_EXPERT = 64
N_FSDP = 8


def steps_of(own_key, extent, split, smallest, high):
    factor_of = 1.0
    for position, blocks in split:
        heights = jax.random.uniform(jax.random.fold_in(jax.random.fold_in(own_key, 6), position), (blocks,), jnp.float32, smallest / len(split), high / len(split))
        factor_of = factor_of * jnp.repeat(jnp.exp(heights), extent[position] // blocks).reshape((-1,) + (1,) * (len(extent) - 1 - position))
    return factor_of


def deal_out(stream_key, own, number, rows, count, top, bound, slope):
    sequence = jax.random.permutation(stream_key, count)
    crowded, common = load_shares(count, rows * top, bound, slope, True), load_shares(count, rows * top, bound, slope, False)
    places = jnp.arange(count)

    def named(tallies, rotation):
        used = int((tallies > 0).sum())
        fixed = max(1, used // 4)
        passed = fixed + (places - fixed + rotation * (used - fixed)) % max(1, count - fixed)
        return jnp.zeros((count,), jnp.int32).at[sequence[jnp.where(places < fixed, places, passed)]].set(jnp.asarray(tallies, jnp.int32))

    tallies = jnp.where(number % 4 == 0, named(crowded, number // 4), named(common, number - number // 4 - 1))
    mixed = jax.random.permutation(jax.random.fold_in(own, 3), count)
    giver, sink = mixed[0:count // 2 * 2:2], mixed[1:count // 2 * 2:2]
    margin = jnp.minimum(tallies[giver] - 1, bound - tallies[sink]) // 2
    margin = jnp.where((giver == sequence[0]) | (sink == sequence[0]) | (tallies[sink] == 0), 0, jnp.maximum(margin, 0))
    passed = jax.random.randint(jax.random.fold_in(own, 4), (count // 2,), 0, 1 << 20) % (margin + 1)
    tallies = tallies.at[giver].add(-passed).at[sink].add(passed)
    members = jnp.searchsorted(jnp.cumsum(tallies), jnp.arange(rows * top), side="right").astype(jnp.int32)
    grid = members.reshape(top, rows).T
    grid = grid[jax.random.permutation(jax.random.fold_in(own, 1), rows)]
    rotation = jax.random.randint(jax.random.fold_in(own, 2), (rows, 1), 0, top)
    return jnp.take_along_axis(grid, (jnp.arange(top)[None, :] + rotation) % top, axis=1)


def load_shares(number_of, total, reach, slope, full):
    loads = [(1 << 20) // math.isqrt(grade ** slope) + 1 for grade in range(1, number_of + 1)]
    largest = reach if full else min(reach, max(-(-total // number_of), total * loads[0] // sum(loads)))
    least = 1 if total - largest >= number_of - 1 else 0
    counts, rest = [largest] + [least] * (number_of - 1), total - largest - least * (number_of - 1)
    while rest > 0:
        candidates = [i for i in range(1, number_of) if counts[i] < largest] or [i for i in range(1, number_of) if counts[i] < reach]
        pool, budget = sum([loads[i] for i in candidates]), rest
        for i in candidates:
            extra = min(reach - counts[i], max(1, budget * loads[i] // pool), rest)
            counts[i] = counts[i] + extra
            rest = rest - extra
    return np.array(counts)


def scatter_about(own_key, dims, deviation, reach, pieces=(), kind=jnp.bfloat16):
    loudness = steps_of(own_key, dims, pieces, -0.22, 0.18) if pieces else 1.0
    entries = jax.random.normal(own_key, dims, jnp.float32) * deviation * loudness
    return jnp.minimum(jnp.maximum(entries, -reach), reach).astype(kind)


def setup_inputs(seed: int = 0) -> dict:
    keys = jax.random.split(jax.random.key(seed), 8)
    tokens = scatter_about(keys[0], (TOKENS, D), 1.0, 6.0, ((0, 64), (1, 8)))
    expert_ids_keys = jax.random.split(jax.random.fold_in(keys[1], 1), TOKENS // TOK_DEV)
    expert_ids_turns = jax.random.permutation(jax.random.fold_in(keys[1], 3), TOKENS // TOK_DEV)
    expert_ids = jax.vmap(lambda own, number: deal_out(jax.random.fold_in(keys[1], 2), own, number, TOK_DEV, EXPERTS, TOP, MOST, 2))(expert_ids_keys, expert_ids_turns).reshape((TOKENS, TOP))
    route_logits = scatter_about(keys[2], (TOKENS, TOP), 1.5, 6.0, ((0, 64),), jnp.float32)
    w_gate = scatter_about(keys[3], (D, EXPERTS * FF), D ** -0.5, 0.078125, ((0, 8), (1, 64)))
    w_up = scatter_about(keys[4], (D, EXPERTS * FF), D ** -0.5, 0.078125, ((0, 8), (1, 64)))
    w_down = scatter_about(keys[5], (EXPERTS * FF, D), FF ** -0.5, 0.0625, ((0, 64), (1, 8)))
    out_grad = scatter_about(keys[6], (TOKENS, D), 1.0, 6.0, ((0, 64), (1, 8)))
    return dict(tokens=tokens, expert_ids=expert_ids, route_logits=route_logits, w_gate=w_gate, w_up=w_up, w_down=w_down, out_grad=out_grad)


def as_wire(value):
    narrow = lax.optimization_barrier(value.astype(jnp.bfloat16))
    return narrow.astype(jnp.float32)


def feature_sum(left, right):
    slice_width = D // N_FSDP
    total = jnp.zeros((left.shape[0], right.shape[1]), jnp.float32)
    for index in range(N_FSDP):
        partial_sum = jnp.dot(left[:, index * slice_width:(index + 1) * slice_width], right[index * slice_width:(index + 1) * slice_width, :], preferred_element_type=jnp.float32)
        total = total + as_wire(partial_sum)
    return total


def reference(tokens, expert_ids, route_logits, w_gate, w_up, w_down, out_grad):
    group = N_EXPERT // EXPERTS
    piece = FF // group
    first = jax.nn.sigmoid(route_logits[:, 0] - route_logits[:, 1])
    route_weight = jnp.stack([first, 1.0 - first], axis=1)
    cot = out_grad.astype(jnp.float32)
    route_out = jnp.zeros((TOKENS, TOP, D), jnp.float32)
    tokens_cot = jnp.zeros((TOKENS, D), jnp.float32)
    gate_parts = []
    up_parts = []
    down_parts = []
    for expert in range(EXPERTS):
        w_g = w_gate[:, expert * FF:(expert + 1) * FF]
        w_u = w_up[:, expert * FF:(expert + 1) * FF]
        w_d = w_down[expert * FF:(expert + 1) * FF, :]
        chosen = expert_ids == expert
        routed = jnp.any(chosen, axis=1)
        scale = jnp.sum(jnp.where(chosen, route_weight, 0.0), axis=1)
        rows = jnp.where(routed[:, None], tokens, jnp.zeros_like(tokens))
        gate = feature_sum(rows, w_g)
        upper = feature_sum(rows, w_u)
        sig = jax.nn.sigmoid(gate)
        hidden = (gate * sig * upper).astype(jnp.bfloat16)
        route_cot = (scale[:, None] * cot).astype(jnp.bfloat16)
        hidden_cot = feature_sum(route_cot, w_d.T)
        gate_cot = (hidden_cot * upper * sig * (1.0 + gate * (1.0 - sig))).astype(jnp.bfloat16)
        up_cot = (hidden_cot * gate * sig).astype(jnp.bfloat16)
        output = jnp.zeros((TOKENS, D), jnp.float32)
        for index in range(group):
            low = index * piece
            high = (index + 1) * piece
            term = jnp.dot(hidden[:, low:high], w_d[low:high, :], preferred_element_type=jnp.float32)
            output = output + as_wire(term)
            back = lax.dot_general(gate_cot[:, low:high], w_g[:, low:high], (((1,), (1,)), ((), ())), preferred_element_type=jnp.float32)
            back = back + lax.dot_general(up_cot[:, low:high], w_u[:, low:high], (((1,), (1,)), ((), ())), preferred_element_type=jnp.float32)
            tokens_cot = tokens_cot + jnp.where(routed[:, None], as_wire(back), 0.0)
        route_out = route_out + jnp.where(chosen[:, :, None], output[:, None, :], 0.0)
        gate_parts.append(lax.dot_general(rows, gate_cot, (((0,), (0,)), ((), ())), preferred_element_type=jnp.float32).astype(jnp.bfloat16))
        up_parts.append(lax.dot_general(rows, up_cot, (((0,), (0,)), ((), ())), preferred_element_type=jnp.float32).astype(jnp.bfloat16))
        down_parts.append(lax.dot_general(hidden, route_cot, (((0,), (0,)), ((), ())), preferred_element_type=jnp.float32).astype(jnp.bfloat16))
    layer_out = jnp.sum(route_weight[:, :, None] * route_out, axis=1).astype(jnp.bfloat16)
    weight_cot = jnp.sum(cot[:, None, :] * route_out, axis=2)
    change = (weight_cot[:, 0] - weight_cot[:, 1]) * first * (1.0 - first)
    logits_grad = jnp.stack([change, -change], axis=1)
    gate_grad = jnp.concatenate(gate_parts, axis=1)
    up_grad = jnp.concatenate(up_parts, axis=1)
    down_grad = jnp.concatenate(down_parts, axis=0)
    return (layer_out, tokens_cot.astype(jnp.bfloat16), gate_grad, up_grad, down_grad, logits_grad)
```

```python
import jax
import jax.numpy as jnp
from jax import lax
from jax.sharding import PartitionSpec as P

EXPERTS = 4
MOST = 10
CORES = 2
LANES = 128


def contract(left, right, left_dim, right_dim):
    return lax.dot_general(
        left, right, (((left_dim,), (right_dim,)), ((), ())), preferred_element_type=jnp.float32
    )


def on_device(tokens, expert_ids, route_logits, w_gate, w_up, w_down, out_grad):
    count, width = tokens.shape
    hidden_width = w_gate.shape[1]
    peers = lax.axis_size("expert")
    planes = lax.axis_size("fsdp")
    chips = peers // CORES
    slab = MOST * width // LANES
    half = chips * MOST
    rows = CORES * half
    own = rows // planes
    same_core = [[CORES * p + c for p in range(chips)] for c in range(CORES)]
    other_core = [(i, i ^ 1) for i in range(peers)]

    def across_chips(blocks):
        return lax.all_to_all(
            blocks, "expert", split_axis=0, concat_axis=0, axis_index_groups=same_core, tiled=True
        )

    def swap(value):
        return lax.ppermute(value, "expert", other_core)

    def across_planes(blocks):
        return lax.all_to_all(blocks, "fsdp", split_axis=0, concat_axis=0, tiled=True)

    experts = jnp.arange(EXPERTS, dtype=jnp.int32)
    named = expert_ids[:, :, None] == experts[None, None, :]
    chosen = jnp.any(named, axis=1)
    before = jnp.arange(count)[:, None, None] < jnp.arange(count)[None, :, None]
    rank = jnp.sum((before & chosen[:, None, :]).astype(jnp.int32), axis=0)
    first = jax.nn.sigmoid(route_logits[:, 0] - route_logits[:, 1])
    route_weight = jnp.stack([first, 1.0 - first], axis=1)
    scale = jnp.sum(jnp.where(named, route_weight[:, :, None], 0.0), axis=1)
    slots = jnp.arange(MOST, dtype=jnp.int32)
    picked = (chosen.T[:, None, :]) & (rank.T[:, None, :] == slots[None, :, None])
    select = picked.reshape(EXPERTS * MOST, count)
    slot_scale = jnp.sum(
        jnp.where(picked, scale.T[:, None, :], 0.0), axis=2
    ).reshape(EXPERTS * MOST, 1)
    token_slots = contract(select.astype(jnp.bfloat16), tokens, 1, 0).astype(jnp.bfloat16)
    cot_slots = (slot_scale * contract(select.astype(jnp.bfloat16), out_grad, 1, 0)).astype(
        jnp.bfloat16
    )

    def blocks_for_all(slot_rows):
        blocks = slot_rows.reshape(EXPERTS, slab, LANES)
        return jnp.repeat(blocks, chips // EXPERTS, axis=0)

    def rows_of(blocks):
        return blocks.reshape(half, width)

    def gather_rows(slot_rows):
        mine = across_chips(blocks_for_all(slot_rows))
        return jnp.concatenate([rows_of(mine), rows_of(swap(mine))], axis=0)

    def give_back(part):
        mine = part[:half].astype(jnp.float32) + swap(part[half:]).astype(jnp.float32)
        sent = mine.astype(jnp.bfloat16).reshape(chips, slab, LANES)
        back = across_chips(sent).astype(jnp.float32)
        return (
            back.reshape(EXPERTS, chips // EXPERTS, slab, LANES)
            .sum(axis=1)
            .reshape(EXPERTS * MOST, width)
        )

    def plane_sum(parts):
        return across_planes(parts.reshape(planes, own, -1)).astype(jnp.float32).sum(axis=0)

    def to_all_planes(value):
        copies = jnp.broadcast_to(value[None], (planes,) + value.shape)
        return across_planes(copies).reshape(rows, -1)

    arrived = gather_rows(token_slots)
    arrived_cot = gather_rows(cot_slots)
    gate_part = jnp.dot(arrived, w_gate, preferred_element_type=jnp.float32).astype(jnp.bfloat16)
    up_part = jnp.dot(arrived, w_up, preferred_element_type=jnp.float32).astype(jnp.bfloat16)
    both = plane_sum(jnp.concatenate([gate_part, up_part], axis=1))
    gate, upper = both[:, :hidden_width], both[:, hidden_width:]
    sig = jax.nn.sigmoid(gate)
    hidden_own = (gate * sig * upper).astype(jnp.bfloat16)
    hidden_cot = plane_sum(contract(arrived_cot, w_down, 1, 1).astype(jnp.bfloat16))
    gate_cot_own = (hidden_cot * upper * sig * (1.0 + gate * (1.0 - sig))).astype(jnp.bfloat16)
    up_cot_own = (hidden_cot * gate * sig).astype(jnp.bfloat16)
    hidden = to_all_planes(hidden_own)
    cots = to_all_planes(jnp.concatenate([gate_cot_own, up_cot_own], axis=1))
    gate_cot, up_cot = cots[:, :hidden_width], cots[:, hidden_width:]

    out_part = jnp.dot(hidden, w_down, preferred_element_type=jnp.float32).astype(jnp.bfloat16)
    out_slots = give_back(out_part)
    tokens_part = (contract(gate_cot, w_gate, 1, 1) + contract(up_cot, w_up, 1, 1)).astype(
        jnp.bfloat16
    )
    grad_slots = give_back(tokens_part)
    down_grad = contract(hidden, arrived_cot, 0, 0).astype(jnp.bfloat16)
    gate_grad = contract(arrived, gate_cot, 0, 0).astype(jnp.bfloat16)
    up_grad = contract(arrived, up_cot, 0, 0).astype(jnp.bfloat16)

    rank_of_route = jnp.sum(jnp.where(named, rank[:, None, :], 0), axis=2)
    place = (expert_ids * MOST + rank_of_route).reshape(-1)
    route_out = jnp.take(out_slots, place, axis=0).reshape(count, -1, width)
    layer_out = jnp.sum(route_weight[:, :, None] * route_out, axis=1).astype(jnp.bfloat16)
    route_grad = jnp.take(grad_slots, place, axis=0).reshape(count, -1, width)
    tokens_grad = jnp.sum(route_grad, axis=1).astype(jnp.bfloat16)
    local_products = jnp.sum(out_grad.astype(jnp.float32)[:, None, :] * route_out, axis=2)
    copies = jnp.broadcast_to(local_products[None], (planes,) + local_products.shape)
    weight_cot = across_planes(copies).sum(axis=0)
    change = (weight_cot[:, 0] - weight_cot[:, 1]) * first * (1.0 - first)
    logits_grad = jnp.stack([change, -change], axis=1)
    return (layer_out, tokens_grad, gate_grad, up_grad, down_grad, logits_grad)


def solution(mesh):
    return jax.shard_map(
        on_device,
        mesh=mesh,
        in_specs=(
            P("expert", "fsdp"),
            P("expert", None),
            P("expert", None),
            P("fsdp", "expert"),
            P("fsdp", "expert"),
            P("expert", "fsdp"),
            P("expert", "fsdp"),
        ),
        out_specs=(
            P("expert", "fsdp"),
            P("expert", "fsdp"),
            P("fsdp", "expert"),
            P("fsdp", "expert"),
            P("expert", "fsdp"),
            P("expert", None),
        ),
        check_vma=False,
    )
```

```python
import jax
import jax.numpy as jnp
from jax import lax
from jax.sharding import PartitionSpec as P

EXPERTS = 4
MOST = 10
CORES = 2
LANES = 128


def contract(left, right, left_dim, right_dim):
    return lax.dot_general(
        left, right, (((left_dim,), (right_dim,)), ((), ())), preferred_element_type=jnp.float32
    )


def on_device(tokens, expert_ids, route_logits, w_gate, w_up, w_down, out_grad):
    count, width = tokens.shape
    hidden_width = w_gate.shape[1]
    peers = lax.axis_size("expert")
    planes = lax.axis_size("fsdp")
    chips = peers // CORES
    slab = MOST * width // LANES
    half = chips * MOST
    rows = CORES * half
    own = rows // planes
    same_core = [[CORES * p + c for p in range(chips)] for c in range(CORES)]
    other_core = [(i, i ^ 1) for i in range(peers)]

    def across_chips(blocks):
        return lax.all_to_all(
            blocks, "expert", split_axis=0, concat_axis=0, axis_index_groups=same_core, tiled=True
        )

    def swap(value):
        return lax.ppermute(value, "expert", other_core)

    def across_planes(blocks):
        return lax.all_to_all(blocks, "fsdp", split_axis=0, concat_axis=0, tiled=True)

    def after(value, *earlier):
        return lax.optimization_barrier((value,) + earlier)[0]

    experts = jnp.arange(EXPERTS, dtype=jnp.int32)
    named = expert_ids[:, :, None] == experts[None, None, :]
    chosen = jnp.any(named, axis=1)
    before = jnp.arange(count)[:, None, None] < jnp.arange(count)[None, :, None]
    rank = jnp.sum((before & chosen[:, None, :]).astype(jnp.int32), axis=0)
    first = jax.nn.sigmoid(route_logits[:, 0] - route_logits[:, 1])
    route_weight = jnp.stack([first, 1.0 - first], axis=1)
    scale = jnp.sum(jnp.where(named, route_weight[:, :, None], 0.0), axis=1)
    slots = jnp.arange(MOST, dtype=jnp.int32)
    picked = (chosen.T[:, None, :]) & (rank.T[:, None, :] == slots[None, :, None])
    select = picked.reshape(EXPERTS * MOST, count)
    slot_scale = jnp.sum(
        jnp.where(picked, scale.T[:, None, :], 0.0), axis=2
    ).reshape(EXPERTS * MOST, 1)
    token_slots = contract(select.astype(jnp.bfloat16), tokens, 1, 0).astype(jnp.bfloat16)
    cot_slots = (slot_scale * contract(select.astype(jnp.bfloat16), out_grad, 1, 0)).astype(
        jnp.bfloat16
    )

    def blocks_for_all(slot_rows):
        blocks = slot_rows.reshape(EXPERTS, slab, LANES)
        return jnp.repeat(blocks, chips // EXPERTS, axis=0)

    def rows_of(blocks):
        return blocks.reshape(half, width)

    def gather_rows(slot_rows):
        mine = across_chips(blocks_for_all(slot_rows))
        return jnp.concatenate([rows_of(mine), rows_of(swap(mine))], axis=0)

    def give_back(part):
        mine = part[:half].astype(jnp.float32) + swap(part[half:]).astype(jnp.float32)
        sent = mine.astype(jnp.bfloat16).reshape(chips, slab, LANES)
        back = across_chips(sent).astype(jnp.float32)
        return (
            back.reshape(EXPERTS, chips // EXPERTS, slab, LANES)
            .sum(axis=1)
            .reshape(EXPERTS * MOST, width)
        )

    def plane_sum(parts):
        return across_planes(parts.reshape(planes, own, -1)).astype(jnp.float32).sum(axis=0)

    def to_all_planes(value):
        copies = jnp.broadcast_to(value[None], (planes,) + value.shape)
        return across_planes(copies).reshape(rows, -1)

    arrived = gather_rows(token_slots)
    gate_part = jnp.dot(arrived, w_gate, preferred_element_type=jnp.float32).astype(jnp.bfloat16)
    up_part = jnp.dot(arrived, w_up, preferred_element_type=jnp.float32).astype(jnp.bfloat16)
    parts = jnp.concatenate([gate_part, up_part], axis=1)
    both = lax.psum_scatter(parts, "fsdp", scatter_dimension=0, tiled=True).astype(jnp.float32)

    arrived_cot = gather_rows(after(cot_slots, parts))
    hidden_cot = plane_sum(contract(arrived_cot, w_down, 1, 1).astype(jnp.bfloat16))
    both = after(both, hidden_cot)
    gate, upper = both[:, :hidden_width], both[:, hidden_width:]
    sig = jax.nn.sigmoid(gate)
    hidden_own = (gate * sig * upper).astype(jnp.bfloat16)
    gate_cot_own = (hidden_cot * upper * sig * (1.0 + gate * (1.0 - sig))).astype(jnp.bfloat16)
    up_cot_own = (hidden_cot * gate * sig).astype(jnp.bfloat16)
    cots_own = jnp.concatenate([gate_cot_own, up_cot_own], axis=1)
    cots = lax.all_gather(cots_own, "fsdp", axis=0, tiled=True)

    hidden = to_all_planes(after(hidden_own, cots_own))
    out_part = jnp.dot(hidden, w_down, preferred_element_type=jnp.float32).astype(jnp.bfloat16)
    out_slots = give_back(out_part)
    down_grad = contract(hidden, arrived_cot, 0, 0).astype(jnp.bfloat16)

    gate_cot, up_cot = cots[:, :hidden_width], cots[:, hidden_width:]
    tokens_part = (contract(gate_cot, w_gate, 1, 1) + contract(up_cot, w_up, 1, 1)).astype(
        jnp.bfloat16
    )
    grad_slots = give_back(tokens_part)
    gate_grad = contract(arrived, gate_cot, 0, 0).astype(jnp.bfloat16)
    up_grad = contract(arrived, up_cot, 0, 0).astype(jnp.bfloat16)

    rank_of_route = jnp.sum(jnp.where(named, rank[:, None, :], 0), axis=2)
    place = after((expert_ids * MOST + rank_of_route).reshape(-1), tokens_part)
    route_out = jnp.take(out_slots, place, axis=0).reshape(count, -1, width)
    layer_out = jnp.sum(route_weight[:, :, None] * route_out, axis=1).astype(jnp.bfloat16)
    local_products = jnp.sum(out_grad.astype(jnp.float32)[:, None, :] * route_out, axis=2)
    copies = jnp.broadcast_to(local_products[None], (planes,) + local_products.shape)
    weight_cot = across_planes(copies).sum(axis=0)
    route_grad = jnp.take(after(grad_slots, weight_cot), place, axis=0).reshape(count, -1, width)
    tokens_grad = jnp.sum(route_grad, axis=1).astype(jnp.bfloat16)
    change = (weight_cot[:, 0] - weight_cot[:, 1]) * first * (1.0 - first)
    logits_grad = jnp.stack([change, -change], axis=1)
    return (layer_out, tokens_grad, gate_grad, up_grad, down_grad, logits_grad)


def solution(mesh):
    return jax.shard_map(
        on_device,
        mesh=mesh,
        in_specs=(
            P("expert", "fsdp"),
            P("expert", None),
            P("expert", None),
            P("fsdp", "expert"),
            P("fsdp", "expert"),
            P("expert", "fsdp"),
            P("expert", "fsdp"),
        ),
        out_specs=(
            P("expert", "fsdp"),
            P("expert", "fsdp"),
            P("fsdp", "expert"),
            P("fsdp", "expert"),
            P("expert", "fsdp"),
            P("expert", None),
        ),
        check_vma=False,
    )
```

```python
import jax
import jax.numpy as jnp
from jax import lax
from jax.sharding import PartitionSpec as P

EXPERTS = 4
MOST = 10
CORES = 2
LANES = 128


def contract(left, right, left_dim, right_dim):
    return lax.dot_general(
        left, right, (((left_dim,), (right_dim,)), ((), ())), preferred_element_type=jnp.float32
    )


def on_device(tokens, expert_ids, route_logits, w_gate, w_up, w_down, out_grad):
    count, width = tokens.shape
    hidden_width = w_gate.shape[1]
    peers = lax.axis_size("expert")
    planes = lax.axis_size("fsdp")
    group = peers // EXPERTS
    chips = group // CORES
    half = peers // CORES * MOST
    rows = CORES * half
    own = rows // planes
    matching = [[group * e + i for e in range(EXPERTS)] for i in range(group)]
    same_core = [
        [group * e + CORES * p + c for p in range(chips)]
        for e in range(EXPERTS)
        for c in range(CORES)
    ]
    other_core = [(i, i ^ 1) for i in range(peers)]

    def across(blocks, groups):
        return lax.all_to_all(
            blocks, "expert", split_axis=0, concat_axis=0, axis_index_groups=groups, tiled=True
        )

    def swap(value):
        return lax.ppermute(value, "expert", other_core)

    experts = jnp.arange(EXPERTS, dtype=jnp.int32)
    named = expert_ids[:, :, None] == experts[None, None, :]
    chosen = jnp.any(named, axis=1)
    before = jnp.arange(count)[:, None, None] < jnp.arange(count)[None, :, None]
    rank = jnp.sum((before & chosen[:, None, :]).astype(jnp.int32), axis=0)
    first = jax.nn.sigmoid(route_logits[:, 0] - route_logits[:, 1])
    route_weight = jnp.stack([first, 1.0 - first], axis=1)
    scale = jnp.sum(jnp.where(named, route_weight[:, :, None], 0.0), axis=1)
    slots = jnp.arange(MOST, dtype=jnp.int32)
    picked = (chosen.T[:, None, :]) & (rank.T[:, None, :] == slots[None, :, None])
    select = picked.reshape(EXPERTS * MOST, count)
    slot_scale = jnp.sum(
        jnp.where(picked, scale.T[:, None, :], 0.0), axis=2
    ).reshape(EXPERTS * MOST, 1)
    token_slots = contract(select.astype(jnp.bfloat16), tokens, 1, 0).astype(jnp.bfloat16)
    cot_slots = (slot_scale * contract(select.astype(jnp.bfloat16), out_grad, 1, 0)).astype(
        jnp.bfloat16
    )

    def gather_rows(slot_rows):
        mine = across(slot_rows.reshape(EXPERTS, -1, LANES), matching)
        copies = jnp.broadcast_to(mine.reshape(1, -1, LANES), (chips, mine.size // LANES, LANES))
        arrived = across(copies, same_core)
        return jnp.concatenate(
            [arrived.reshape(half, -1), swap(arrived).reshape(half, -1)], axis=0
        )

    def shift(value, by):
        pairs = [(i, (i + by) % planes) for i in range(planes)]
        return lax.ppermute(value, "fsdp", pairs)

    def shift_by_core(value, by):
        pairs = []
        for e in range(peers):
            for z in range(planes):
                there = (z + by) % planes if e % CORES == 0 else (z - by) % planes
                pairs.append((e * planes + z, e * planes + there))
        return lax.ppermute(value, ("expert", "fsdp"), pairs)

    me = lax.axis_index("expert")
    plane = lax.axis_index("fsdp")
    even_core = me % CORES == 0

    def plane_sum(parts):
        chunks = parts.reshape(planes, own, -1)

        def chunk(ahead):
            at = (plane + ahead + planes) % planes
            return lax.dynamic_slice_in_dim(chunks, at, 1, axis=0)[0]

        def wide(value):
            return value.astype(jnp.float32)

        up_three = shift(chunk(3), 1)
        down_three = shift(chunk(-3), -1)
        four = wide(shift_by_core(chunk(4), 2))
        up_one = shift(chunk(1), 1)
        down_one = shift(chunk(-1), -1)
        up_two = wide(chunk(2)) + wide(up_three) + jnp.where(even_core, four, 0.0)
        down_two = wide(chunk(-2)) + wide(down_three) + jnp.where(even_core, 0.0, four)
        up_two = shift(up_two.astype(jnp.bfloat16), 2)
        down_two = shift(down_two.astype(jnp.bfloat16), -2)
        near = wide(chunk(0)) + wide(up_one) + wide(down_one)
        return near + wide(up_two) + wide(down_two)

    def to_all_planes(value):
        next_two, last_two = shift(value, -2), shift(value, 2)
        next_one, last_one = shift(value, -1), shift(value, 1)
        four = shift_by_core(jnp.where(even_core, next_two, last_two), -2)
        next_three, last_three = shift(next_two, -1), shift(last_two, 1)
        chunks = jnp.zeros((planes,) + value.shape, value.dtype)
        order = [value, next_one, next_two, next_three, four, last_three, last_two, last_one]
        for ahead, piece in enumerate(order):
            at = (plane + ahead) % planes
            chunks = lax.dynamic_update_slice_in_dim(chunks, piece[None], at, axis=0)
        return chunks.reshape(rows, -1)

    def two_columns(product):
        near = lax.reduce_precision(product, 8, 7)
        far = product - near
        both = jnp.stack([near, far], axis=1).astype(jnp.bfloat16)
        return jnp.pad(both, ((0, 0), (0, LANES - 2)))

    def narrow(summed):
        product = summed[:, -LANES] + summed[:, 1 - LANES]
        return jnp.concatenate(
            [summed[:, :-LANES].astype(jnp.bfloat16), two_columns(product)], axis=1
        )

    def give_back(part):
        mine = narrow(part[:half].astype(jnp.float32) + swap(part[half:]).astype(jnp.float32))
        arrived = across(mine.reshape(chips, -1, LANES), same_core)
        summed = arrived.astype(jnp.float32).sum(axis=0).reshape(EXPERTS * MOST, -1)
        back = across(narrow(summed).reshape(EXPERTS, -1, LANES), matching)
        return back.reshape(EXPERTS * MOST, -1).astype(jnp.float32)

    experts = jnp.arange(EXPERTS, dtype=jnp.int32)
    named = expert_ids[:, :, None] == experts[None, None, :]
    chosen = jnp.any(named, axis=1)
    before = jnp.arange(count)[:, None, None] < jnp.arange(count)[None, :, None]
    rank = jnp.sum((before & chosen[:, None, :]).astype(jnp.int32), axis=0)
    first = jax.nn.sigmoid(route_logits[:, 0] - route_logits[:, 1])
    route_weight = jnp.stack([first, 1.0 - first], axis=1)
    scale = jnp.sum(jnp.where(named, route_weight[:, :, None], 0.0), axis=1)
    slots = jnp.arange(MOST, dtype=jnp.int32)
    picked = (chosen.T[:, None, :]) & (rank.T[:, None, :] == slots[None, :, None])
    select = picked.reshape(EXPERTS * MOST, count)
    slot_scale = jnp.sum(
        jnp.where(picked, scale.T[:, None, :], 0.0), axis=2
    ).reshape(EXPERTS * MOST, 1)
    token_slots = contract(select.astype(jnp.bfloat16), tokens, 1, 0).astype(jnp.bfloat16)
    cot_slots = (slot_scale * contract(select.astype(jnp.bfloat16), out_grad, 1, 0)).astype(
        jnp.bfloat16
    )

    def gather_rows(slot_rows):
        mine = across(slot_rows.reshape(EXPERTS, -1, LANES), matching)
        copies = jnp.broadcast_to(mine.reshape(1, -1, LANES), (chips, mine.size // LANES, LANES))
        arrived = across(copies, same_core)
        return jnp.concatenate(
            [arrived.reshape(half, -1), swap(arrived).reshape(half, -1)], axis=0
        )

    def give_back(part):
        mine = part[:half].astype(jnp.float32) + swap(part[half:]).astype(jnp.float32)
        sent = mine.astype(jnp.bfloat16).reshape(chips, -1, LANES)
        summed = across(sent, same_core).astype(jnp.float32).sum(axis=0).astype(jnp.bfloat16)
        back = across(summed.reshape(EXPERTS, -1, LANES), matching)
        return back.reshape(EXPERTS * MOST, -1).astype(jnp.float32)

    both = gather_rows(jnp.concatenate([token_slots, cot_slots], axis=1))
    arrived, arrived_cot = both[:, :width], both[:, width:]
    parts = jnp.concatenate(
        [
            jnp.dot(arrived, w_gate, preferred_element_type=jnp.float32).astype(jnp.bfloat16),
            jnp.dot(arrived, w_up, preferred_element_type=jnp.float32).astype(jnp.bfloat16),
            contract(arrived_cot, w_down, 1, 1).astype(jnp.bfloat16),
        ],
        axis=1,
    )
    sums = plane_sum(parts)
    gate = sums[:, :hidden_width]
    upper = sums[:, hidden_width : 2 * hidden_width]
    hidden_cot = sums[:, 2 * hidden_width :]
    sig = jax.nn.sigmoid(gate)
    hidden_own = (gate * sig * upper).astype(jnp.bfloat16)
    gate_cot_own = (hidden_cot * upper * sig * (1.0 + gate * (1.0 - sig))).astype(jnp.bfloat16)
    up_cot_own = (hidden_cot * gate * sig).astype(jnp.bfloat16)
    product = jnp.sum(hidden_own.astype(jnp.float32) * hidden_cot, axis=1)
    gathered = to_all_planes(
        jnp.concatenate([hidden_own, gate_cot_own, up_cot_own, two_columns(product)], axis=1)
    )
    hidden = gathered[:, :hidden_width]
    gate_cot = gathered[:, hidden_width : 2 * hidden_width]
    up_cot = gathered[:, 2 * hidden_width : 3 * hidden_width]

    tokens_part = contract(gate_cot, w_gate, 1, 1) + contract(up_cot, w_up, 1, 1)
    out_part = jnp.dot(hidden, w_down, preferred_element_type=jnp.float32)
    back = give_back(
        jnp.concatenate(
            [
                out_part.astype(jnp.bfloat16),
                tokens_part.astype(jnp.bfloat16),
                gathered[:, 3 * hidden_width :],
            ],
            axis=1,
        )
    )
    out_slots, grad_slots = back[:, :width], back[:, width : 2 * width]
    slot_products = back[:, 2 * width] + back[:, 2 * width + 1]
    down_grad = contract(hidden, arrived_cot, 0, 0).astype(jnp.bfloat16)
    gate_grad = contract(arrived, gate_cot, 0, 0).astype(jnp.bfloat16)
    up_grad = contract(arrived, up_cot, 0, 0).astype(jnp.bfloat16)

    rank_of_route = jnp.sum(jnp.where(named, rank[:, None, :], 0), axis=2)
    place = expert_ids * MOST + rank_of_route
    route_product = jnp.sum(
        jnp.where(
            place[:, :, None] == jnp.arange(EXPERTS * MOST)[None, None, :], slot_products, 0.0
        ),
        axis=2,
    )
    route_out = jnp.take(out_slots, place.reshape(-1), axis=0).reshape(count, -1, width)
    layer_out = jnp.sum(route_weight[:, :, None] * route_out, axis=1).astype(jnp.bfloat16)
    route_grad = jnp.take(grad_slots, place.reshape(-1), axis=0).reshape(count, -1, width)
    tokens_grad = jnp.sum(route_grad, axis=1).astype(jnp.bfloat16)
    change = route_product[:, 0] * route_weight[:, 1] - route_product[:, 1] * route_weight[:, 0]
    logits_grad = jnp.stack([change, -change], axis=1)
    return (layer_out, tokens_grad, gate_grad, up_grad, down_grad, logits_grad)


def solution(mesh):
    return jax.shard_map(
        on_device,
        mesh=mesh,
        in_specs=(
            P("expert", "fsdp"),
            P("expert", None),
            P("expert", None),
            P("fsdp", "expert"),
            P("fsdp", "expert"),
            P("expert", "fsdp"),
            P("expert", "fsdp"),
        ),
        out_specs=(
            P("expert", "fsdp"),
            P("expert", "fsdp"),
            P("fsdp", "expert"),
            P("fsdp", "expert"),
            P("expert", "fsdp"),
            P("expert", None),
        ),
        check_vma=False,
    )
```

```python
import jax
import jax.numpy as jnp
from jax import lax
from jax.experimental import pallas as pl
from jax.experimental.pallas import tpu as pltpu
from jax.sharding import PartitionSpec as P

EXPERTS = 4
MOST = 10
CORES = 2
LANES = 128


def contract(left, right, left_dim, right_dim):
    return lax.dot_general(
        left, right, (((left_dim,), (right_dim,)), ((), ())), preferred_element_type=jnp.float32
    )


VMEM = pl.BlockSpec(memory_space=pltpu.VMEM)
SMEM = pl.BlockSpec(memory_space=pltpu.SMEM)
PARAMS = pltpu.CompilerParams(vmem_limit_bytes=40 * 1024 * 1024)


def route_masks(ids_ref, logits_ref):
    count = ids_ref.shape[0]
    slots = EXPERTS * MOST
    slot = lax.broadcasted_iota(jnp.int32, (count, slots), 1)
    expert = jnp.zeros((count, slots), jnp.int32)
    for e in range(1, EXPERTS):
        expert = expert + (slot >= e * MOST).astype(jnp.int32)
    named = [ids_ref[:, k : k + 1] == expert for k in range(2)]
    chosen = (named[0] | named[1]).astype(jnp.float32)
    row = lax.broadcasted_iota(jnp.int32, (count, count), 0)
    column = lax.broadcasted_iota(jnp.int32, (count, count), 1)
    before = (column < row).astype(jnp.float32)
    rank = jnp.dot(before, chosen, preferred_element_type=jnp.float32)
    placed = rank == (slot - expert * MOST).astype(jnp.float32)
    masks = [(n & placed).astype(jnp.bfloat16) for n in named]
    first = jax.nn.sigmoid(logits_ref[:, 0:1] - logits_ref[:, 1:2])
    return masks, (first, 1.0 - first)


def pack_kernel(ids_ref, logits_ref, tokens_ref, grad_ref, slots_ref):
    width = tokens_ref.shape[1]
    masks, weights = route_masks(ids_ref, logits_ref)
    grad = grad_ref[...].astype(jnp.float32)
    cots = [(w * grad).astype(jnp.bfloat16) for w in weights]
    slots_ref[:, :width] = contract(masks[0] + masks[1], tokens_ref[...], 0, 0).astype(
        jnp.bfloat16
    )
    slots_ref[:, width:] = (
        contract(masks[0], cots[0], 0, 0) + contract(masks[1], cots[1], 0, 0)
    ).astype(jnp.bfloat16)


def parts_kernel(plane_ref, near_ref, far_ref, gate_ref, up_ref, down_ref, *rest):
    chunks, parts_ref = rest[:-1], rest[-1]
    half = near_ref.shape[0]
    depth, units = gate_ref.shape
    own = chunks[0].shape[0]
    for start, rows_ref in ((0, near_ref), (half, far_ref)):
        rows = rows_ref[:, :depth]
        cots = rows_ref[:, depth:]
        at = slice(start, start + half)
        gate = jnp.dot(rows, gate_ref[...], preferred_element_type=jnp.float32)
        parts_ref[at, :units] = gate.astype(jnp.bfloat16)
        upper = jnp.dot(rows, up_ref[...], preferred_element_type=jnp.float32)
        parts_ref[at, units : 2 * units] = upper.astype(jnp.bfloat16)
        hidden_cot = contract(cots, down_ref[...], 1, 1)
        parts_ref[at, 2 * units :] = hidden_cot.astype(jnp.bfloat16)
    for ahead, chunk_ref in enumerate(chunks):
        at = lax.rem(plane_ref[0] + ahead, len(chunks)) * own
        chunk_ref[...] = parts_ref[pl.ds(pl.multiple_of(at, 16), own), :]


def product_block(product):
    near = product.astype(jnp.bfloat16).astype(jnp.float32)
    lane = lax.broadcasted_iota(jnp.int32, (product.shape[0], LANES), 1)
    block = jnp.where(lane == 0, near, jnp.where(lane == 1, product - near, 0.0))
    return block.astype(jnp.bfloat16)


def store_narrow(ref, summed):
    ref[:, :-LANES] = summed[:, :-LANES].astype(jnp.bfloat16)
    tail = summed[:, -LANES:]
    ref[:, -LANES:] = product_block(tail[:, 0:1] + tail[:, 1:2])


def relay_kernel(core_ref, up_ref, up_three_ref, down_ref, down_three_ref, four_ref, *outs):
    even = core_ref[0] == 0
    four = four_ref[...].astype(jnp.float32)
    up = up_ref[...].astype(jnp.float32) + up_three_ref[...].astype(jnp.float32)
    outs[0][...] = (up + jnp.where(even, four, 0.0)).astype(jnp.bfloat16)
    down = down_ref[...].astype(jnp.float32) + down_three_ref[...].astype(jnp.float32)
    outs[1][...] = (down + jnp.where(even, 0.0, four)).astype(jnp.bfloat16)


def hidden_kernel(a_ref, b_ref, c_ref, d_ref, e_ref, value_ref):
    units = a_ref.shape[1] // 3

    def summed(columns):
        total = a_ref[:, columns].astype(jnp.float32)
        for ref in (b_ref, c_ref, d_ref, e_ref):
            total = total + ref[:, columns].astype(jnp.float32)
        return total

    gate = summed(slice(0, units))
    upper = summed(slice(units, 2 * units))
    hidden_cot = summed(slice(2 * units, 3 * units))
    sig = jax.nn.sigmoid(gate)
    hidden = (gate * sig * upper).astype(jnp.bfloat16)
    value_ref[:, :units] = hidden
    gate_cot = hidden_cot * upper * sig * (1.0 + gate * (1.0 - sig))
    value_ref[:, units : 2 * units] = gate_cot.astype(jnp.bfloat16)
    value_ref[:, 2 * units : 3 * units] = (hidden_cot * gate * sig).astype(jnp.bfloat16)
    product = jnp.sum(hidden.astype(jnp.float32) * hidden_cot, axis=1, keepdims=True)
    value_ref[:, 3 * units :] = product_block(product)


def back_kernel(plane_ref, gate_ref, up_ref, down_ref, *rest):
    pieces, (near_ref, far_ref, hidden_ref, gate_cot_ref, up_cot_ref, tail_ref) = rest[:8], rest[8:]
    own = pieces[0].shape[0]
    half = near_ref.shape[0]
    depth, units = gate_ref.shape
    for ahead, piece in enumerate(pieces):
        at = pl.multiple_of(lax.rem(plane_ref[0] + ahead, len(pieces)) * own, 16)
        at = pl.ds(at, own)
        hidden_ref[at, :] = piece[:, :units]
        gate_cot_ref[at, :] = piece[:, units : 2 * units]
        up_cot_ref[at, :] = piece[:, 2 * units : 3 * units]
        tail_ref[at, :] = piece[:, 3 * units :]
    for start, ref in ((half, far_ref), (0, near_ref)):
        at = slice(start, start + half)
        out = jnp.dot(hidden_ref[at, :], down_ref[...], preferred_element_type=jnp.float32)
        ref[:, :depth] = out.astype(jnp.bfloat16)
        grad = contract(gate_cot_ref[at, :], gate_ref[...], 1, 1)
        grad = grad + contract(up_cot_ref[at, :], up_ref[...], 1, 1)
        ref[:, depth : 2 * depth] = grad.astype(jnp.bfloat16)
        ref[:, 2 * depth :] = tail_ref[at, :]


def add_kernel(near_ref, far_ref, sum_ref):
    store_narrow(sum_ref, near_ref[...].astype(jnp.float32) + far_ref[...].astype(jnp.float32))


def fold_kernel(blocks_ref, sum_ref):
    total = blocks_ref[0].astype(jnp.float32)
    for i in range(1, blocks_ref.shape[0]):
        total = total + blocks_ref[i].astype(jnp.float32)
    store_narrow(sum_ref, total)


def call(kernel, outs, scalars, arrays, scratch=(), flops=0):
    return pl.pallas_call(
        kernel,
        out_shape=[pltpu.VMEM(shape, jnp.bfloat16) for shape in outs],
        in_specs=[SMEM] * len(scalars) + [VMEM] * len(arrays),
        out_specs=[VMEM] * len(outs),
        scratch_shapes=scratch,
        compiler_params=PARAMS,
        cost_estimate=pl.CostEstimate(flops=flops, bytes_accessed=4 << 20, transcendentals=0),
    )(*[value.reshape(1) for value in scalars], *arrays)


def combine_kernel(ids_ref, logits_ref, back_ref, out_ref, tokens_ref, logits_grad_ref):
    width = out_ref.shape[1]
    masks, weights = route_masks(ids_ref, logits_ref)

    def pick(mask, columns):
        return jnp.dot(mask, back_ref[:, columns], preferred_element_type=jnp.float32)

    outs = [pick(m, slice(0, width)) for m in masks]
    out_ref[...] = (weights[0] * outs[0] + weights[1] * outs[1]).astype(jnp.bfloat16)
    tokens_ref[...] = pick(masks[0] + masks[1], slice(width, 2 * width)).astype(jnp.bfloat16)
    products = [pick(m, slice(2 * width, 2 * width + LANES)) for m in masks]
    products = [p[:, 0:1] + p[:, 1:2] for p in products]
    change = products[0] * weights[1] - products[1] * weights[0]
    which = lax.broadcasted_iota(jnp.int32, logits_grad_ref.shape, 1)
    logits_grad_ref[...] = jnp.where(which == 0, change, -change)


def on_device(tokens, expert_ids, route_logits, w_gate, w_up, w_down, out_grad):
    count, width = tokens.shape
    hidden_width = w_gate.shape[1]
    peers = lax.axis_size("expert")
    planes = lax.axis_size("fsdp")
    group = peers // EXPERTS
    chips = group // CORES
    half = peers // CORES * MOST
    rows = CORES * half
    own = rows // planes
    matching = [[group * e + i for e in range(EXPERTS)] for i in range(group)]
    same_core = [
        [group * e + CORES * p + c for p in range(chips)]
        for e in range(EXPERTS)
        for c in range(CORES)
    ]
    other_core = [(i, i ^ 1) for i in range(peers)]

    def across(blocks, groups):
        return lax.all_to_all(
            blocks, "expert", split_axis=0, concat_axis=0, axis_index_groups=groups, tiled=True
        )

    def swap(value):
        return lax.ppermute(value, "expert", other_core)

    def shift(value, by):
        pairs = [(i, (i + by) % planes) for i in range(planes)]
        return lax.ppermute(value, "fsdp", pairs)

    def shift_by_core(value, by):
        pairs = []
        for e in range(peers):
            for z in range(planes):
                there = (z + by) % planes if e % CORES == 0 else (z - by) % planes
                pairs.append((e * planes + z, e * planes + there))
        return lax.ppermute(value, ("expert", "fsdp"), pairs)

    me = lax.axis_index("expert")
    plane = lax.axis_index("fsdp")
    core = me % CORES

    def relay(chunk):
        up_three = shift(chunk[3], 1)
        down_three = shift(chunk[-3], -1)
        four = shift_by_core(chunk[4], 2)
        up_one = shift(chunk[1], 1)
        down_one = shift(chunk[-1], -1)
        arrays = (chunk[2], up_three, chunk[-2], down_three, four)
        up_two, down_two = call(relay_kernel, [four.shape] * 2, [core], arrays)
        return chunk[0], up_one, down_one, shift(up_two, 2), shift(down_two, -2)

    def to_all_planes(value):
        next_two, last_two = shift(value, -2), shift(value, 2)
        next_one, last_one = shift(value, -1), shift(value, 1)
        four = shift_by_core(jnp.where(core == 0, next_two, last_two), -2)
        next_three, last_three = shift(next_two, -1), shift(last_two, 1)
        return value, next_one, next_two, next_three, four, last_three, last_two, last_one

    def gather_rows(slot_rows):
        mine = across(slot_rows.reshape(EXPERTS, -1, LANES), matching)
        mine = mine.reshape(1, EXPERTS * MOST, -1)
        near = across(jnp.broadcast_to(mine, (chips,) + mine.shape[1:]), same_core)
        near = near.reshape(half, -1)
        return near, swap(near)

    def give_back(near, far):
        [mine] = call(add_kernel, [near.shape], [], [near, swap(far)])
        arrived = across(mine.reshape(chips, EXPERTS * MOST, -1), same_core)
        [summed] = call(fold_kernel, [arrived.shape[1:]], [], [arrived])
        back = across(summed.reshape(EXPERTS, -1, LANES), matching)
        return back.reshape(EXPERTS * MOST, -1)

    bf16 = jnp.bfloat16
    [slots] = call(
        pack_kernel,
        [(EXPERTS * MOST, 2 * width)],
        [],
        [expert_ids, route_logits, tokens, out_grad],
    )
    near, far = gather_rows(slots)
    chunks = call(
        parts_kernel,
        [(own, 3 * hidden_width)] * planes,
        [plane],
        [near, far, w_gate, w_up, w_down],
        scratch=[pltpu.VMEM((rows, 3 * hidden_width), bf16)],
        flops=6 * rows * width * hidden_width,
    )
    arrived = jnp.concatenate([near[:, :width], far[:, :width]], axis=0)
    arrived_cot = jnp.concatenate([near[:, width:], far[:, width:]], axis=0)
    [value] = call(hidden_kernel, [(own, 3 * hidden_width + LANES)], [], relay(chunks))
    near_part, far_part, hidden, gate_cot, up_cot = call(
        back_kernel,
        [(half, 2 * width + LANES)] * 2 + [(rows, hidden_width)] * 3,
        [plane],
        [w_gate, w_up, w_down, *to_all_planes(value)],
        scratch=[pltpu.VMEM((rows, LANES), bf16)],
        flops=6 * rows * width * hidden_width,
    )
    back = give_back(near_part, far_part)
    down_grad = contract(hidden, arrived_cot, 0, 0).astype(jnp.bfloat16)
    gate_grad = contract(arrived, gate_cot, 0, 0).astype(jnp.bfloat16)
    up_grad = contract(arrived, up_cot, 0, 0).astype(jnp.bfloat16)

    layer_out, tokens_grad, logits_grad = pl.pallas_call(
        combine_kernel,
        out_shape=[
            jax.ShapeDtypeStruct((count, width), bf16),
            jax.ShapeDtypeStruct((count, width), bf16),
            jax.ShapeDtypeStruct(route_logits.shape, jnp.float32),
        ],
        in_specs=[VMEM] * 3,
        out_specs=[VMEM] * 3,
        compiler_params=PARAMS,
    )(expert_ids, route_logits, back)
    return (layer_out, tokens_grad, gate_grad, up_grad, down_grad, logits_grad)


def solution(mesh):
    return jax.shard_map(
        on_device,
        mesh=mesh,
        in_specs=(
            P("expert", "fsdp"),
            P("expert", None),
            P("expert", None),
            P("fsdp", "expert"),
            P("fsdp", "expert"),
            P("expert", "fsdp"),
            P("expert", "fsdp"),
        ),
        out_specs=(
            P("expert", "fsdp"),
            P("expert", "fsdp"),
            P("fsdp", "expert"),
            P("fsdp", "expert"),
            P("expert", "fsdp"),
            P("expert", None),
        ),
        check_vma=False,
    )
```

```python
import jax
import jax.numpy as jnp
from jax import lax
from jax.experimental import pallas as pl
from jax.experimental.pallas import tpu as pltpu
from jax.sharding import PartitionSpec as P

EXPERTS = 4
MOST = 10
CORES = 2
LANES = 128


def contract(left, right, left_dim, right_dim):
    return lax.dot_general(
        left, right, (((left_dim,), (right_dim,)), ((), ())), preferred_element_type=jnp.float32
    )


VMEM = pl.BlockSpec(memory_space=pltpu.VMEM)
SMEM = pl.BlockSpec(memory_space=pltpu.SMEM)
PARAMS = pltpu.CompilerParams(vmem_limit_bytes=40 * 1024 * 1024)


def route_masks(ids_ref, logits_ref):
    count = ids_ref.shape[0]
    slots = EXPERTS * MOST
    slot = lax.broadcasted_iota(jnp.int32, (count, slots), 1)
    expert = jnp.zeros((count, slots), jnp.int32)
    for e in range(1, EXPERTS):
        expert = expert + (slot >= e * MOST).astype(jnp.int32)
    named = [ids_ref[:, k : k + 1] == expert for k in range(2)]
    chosen = (named[0] | named[1]).astype(jnp.float32)
    row = lax.broadcasted_iota(jnp.int32, (count, count), 0)
    column = lax.broadcasted_iota(jnp.int32, (count, count), 1)
    before = (column < row).astype(jnp.float32)
    rank = jnp.dot(before, chosen, preferred_element_type=jnp.float32)
    placed = rank == (slot - expert * MOST).astype(jnp.float32)
    masks = [(n & placed).astype(jnp.bfloat16) for n in named]
    first = jax.nn.sigmoid(logits_ref[:, 0:1] - logits_ref[:, 1:2])
    return masks, (first, 1.0 - first)


def pack_kernel(ids_ref, logits_ref, tokens_ref, grad_ref, slots_ref):
    width = tokens_ref.shape[1]
    masks, weights = route_masks(ids_ref, logits_ref)
    grad = grad_ref[...].astype(jnp.float32)
    cots = [(w * grad).astype(jnp.bfloat16) for w in weights]
    slots_ref[:, :width] = contract(masks[0] + masks[1], tokens_ref[...], 0, 0).astype(
        jnp.bfloat16
    )
    slots_ref[:, width:] = (
        contract(masks[0], cots[0], 0, 0) + contract(masks[1], cots[1], 0, 0)
    ).astype(jnp.bfloat16)


def load_kernel(*refs):
    count = len(refs) // 2
    copies = [
        pltpu.make_async_copy(refs[i], refs[count + i], refs[2 * count].at[i]) for i in range(count)
    ]
    for copy in copies:
        copy.start()
    for copy in copies:
        copy.wait()


def parts_kernel(plane_ref, near_ref, far_ref, gate_ref, up_ref, down_ref, *rest):
    chunks, parts_ref = rest[:-1], rest[-1]
    half = near_ref.shape[0]
    depth, units = gate_ref.shape
    own = chunks[0].shape[0]
    for start, rows_ref in ((0, near_ref), (half, far_ref)):
        rows = rows_ref[:, :depth]
        cots = rows_ref[:, depth:]
        at = slice(start, start + half)
        gate = jnp.dot(rows, gate_ref[...], preferred_element_type=jnp.float32)
        parts_ref[at, :units] = gate.astype(jnp.bfloat16)
        upper = jnp.dot(rows, up_ref[...], preferred_element_type=jnp.float32)
        parts_ref[at, units : 2 * units] = upper.astype(jnp.bfloat16)
        hidden_cot = contract(cots, down_ref[...], 1, 1)
        parts_ref[at, 2 * units :] = hidden_cot.astype(jnp.bfloat16)
    for ahead, chunk_ref in enumerate(chunks):
        at = lax.rem(plane_ref[0] + ahead, len(chunks)) * own
        chunk_ref[...] = parts_ref[pl.ds(pl.multiple_of(at, 16), own), :]


def product_block(product):
    near = product.astype(jnp.bfloat16).astype(jnp.float32)
    lane = lax.broadcasted_iota(jnp.int32, (product.shape[0], LANES), 1)
    block = jnp.where(lane == 0, near, jnp.where(lane == 1, product - near, 0.0))
    return block.astype(jnp.bfloat16)


def store_narrow(ref, summed):
    ref[:, :-LANES] = summed[:, :-LANES].astype(jnp.bfloat16)
    tail = summed[:, -LANES:]
    ref[:, -LANES:] = product_block(tail[:, 0:1] + tail[:, 1:2])


def relay_kernel(core_ref, up_ref, up_three_ref, down_ref, down_three_ref, four_ref, *outs):
    even = core_ref[0] == 0
    four = four_ref[...].astype(jnp.float32)
    up = up_ref[...].astype(jnp.float32) + up_three_ref[...].astype(jnp.float32)
    outs[0][...] = (up + jnp.where(even, four, 0.0)).astype(jnp.bfloat16)
    down = down_ref[...].astype(jnp.float32) + down_three_ref[...].astype(jnp.float32)
    outs[1][...] = (down + jnp.where(even, 0.0, four)).astype(jnp.bfloat16)


def hidden_kernel(a_ref, b_ref, c_ref, d_ref, e_ref, value_ref):
    units = a_ref.shape[1] // 3

    def summed(columns):
        total = a_ref[:, columns].astype(jnp.float32)
        for ref in (b_ref, c_ref, d_ref, e_ref):
            total = total + ref[:, columns].astype(jnp.float32)
        return total

    gate = summed(slice(0, units))
    upper = summed(slice(units, 2 * units))
    hidden_cot = summed(slice(2 * units, 3 * units))
    sig = jax.nn.sigmoid(gate)
    hidden = (gate * sig * upper).astype(jnp.bfloat16)
    value_ref[:, :units] = hidden
    gate_cot = hidden_cot * upper * sig * (1.0 + gate * (1.0 - sig))
    value_ref[:, units : 2 * units] = gate_cot.astype(jnp.bfloat16)
    value_ref[:, 2 * units : 3 * units] = (hidden_cot * gate * sig).astype(jnp.bfloat16)
    product = jnp.sum(hidden.astype(jnp.float32) * hidden_cot, axis=1, keepdims=True)
    value_ref[:, 3 * units :] = product_block(product)


def back_kernel(plane_ref, gate_ref, up_ref, down_ref, *rest):
    pieces, (near_ref, far_ref, hidden_ref, gate_cot_ref, up_cot_ref, tail_ref) = rest[:8], rest[8:]
    own = pieces[0].shape[0]
    half = near_ref.shape[0]
    depth, units = gate_ref.shape
    for ahead, piece in enumerate(pieces):
        at = pl.multiple_of(lax.rem(plane_ref[0] + ahead, len(pieces)) * own, 16)
        at = pl.ds(at, own)
        hidden_ref[at, :] = piece[:, :units]
        gate_cot_ref[at, :] = piece[:, units : 2 * units]
        up_cot_ref[at, :] = piece[:, 2 * units : 3 * units]
        tail_ref[at, :] = piece[:, 3 * units :]
    for start, ref in ((half, far_ref), (0, near_ref)):
        at = slice(start, start + half)
        out = jnp.dot(hidden_ref[at, :], down_ref[...], preferred_element_type=jnp.float32)
        ref[:, :depth] = out.astype(jnp.bfloat16)
        grad = contract(gate_cot_ref[at, :], gate_ref[...], 1, 1)
        grad = grad + contract(up_cot_ref[at, :], up_ref[...], 1, 1)
        ref[:, depth : 2 * depth] = grad.astype(jnp.bfloat16)
        ref[:, 2 * depth :] = tail_ref[at, :]


def add_kernel(near_ref, far_ref, sum_ref):
    store_narrow(sum_ref, near_ref[...].astype(jnp.float32) + far_ref[...].astype(jnp.float32))


def fold_kernel(blocks_ref, sum_ref):
    total = blocks_ref[0].astype(jnp.float32)
    for i in range(1, blocks_ref.shape[0]):
        total = total + blocks_ref[i].astype(jnp.float32)
    store_narrow(sum_ref, total)


def call(kernel, outs, scalars, arrays, scratch=(), flops=0):
    return pl.pallas_call(
        kernel,
        out_shape=[pltpu.VMEM(shape, jnp.bfloat16) for shape in outs],
        in_specs=[SMEM] * len(scalars) + [VMEM] * len(arrays),
        out_specs=[VMEM] * len(outs),
        scratch_shapes=scratch,
        compiler_params=PARAMS,
        cost_estimate=pl.CostEstimate(flops=flops, bytes_accessed=4 << 20, transcendentals=0),
    )(*[value.reshape(1) for value in scalars], *arrays)


def combine_kernel(ids_ref, logits_ref, back_ref, out_ref, tokens_ref, logits_grad_ref):
    width = out_ref.shape[1]
    masks, weights = route_masks(ids_ref, logits_ref)

    def pick(mask, columns):
        return jnp.dot(mask, back_ref[:, columns], preferred_element_type=jnp.float32)

    outs = [pick(m, slice(0, width)) for m in masks]
    out_ref[...] = (weights[0] * outs[0] + weights[1] * outs[1]).astype(jnp.bfloat16)
    tokens_ref[...] = pick(masks[0] + masks[1], slice(width, 2 * width)).astype(jnp.bfloat16)
    products = [pick(m, slice(2 * width, 2 * width + LANES)) for m in masks]
    products = [p[:, 0:1] + p[:, 1:2] for p in products]
    change = products[0] * weights[1] - products[1] * weights[0]
    which = lax.broadcasted_iota(jnp.int32, logits_grad_ref.shape, 1)
    logits_grad_ref[...] = jnp.where(which == 0, change, -change)


def on_device(tokens, expert_ids, route_logits, w_gate, w_up, w_down, out_grad):
    count, width = tokens.shape
    hidden_width = w_gate.shape[1]
    peers = lax.axis_size("expert")
    planes = lax.axis_size("fsdp")
    group = peers // EXPERTS
    chips = group // CORES
    half = peers // CORES * MOST
    rows = CORES * half
    own = rows // planes
    matching = [[group * e + i for e in range(EXPERTS)] for i in range(group)]
    same_core = [
        [group * e + CORES * p + c for p in range(chips)]
        for e in range(EXPERTS)
        for c in range(CORES)
    ]
    other_core = [(i, i ^ 1) for i in range(peers)]

    def across(blocks, groups):
        return lax.all_to_all(
            blocks, "expert", split_axis=0, concat_axis=0, axis_index_groups=groups, tiled=True
        )

    def swap(value):
        return lax.ppermute(value, "expert", other_core)

    def shift(value, by):
        pairs = [(i, (i + by) % planes) for i in range(planes)]
        return lax.ppermute(value, "fsdp", pairs)

    def shift_by_core(value, by):
        pairs = []
        for e in range(peers):
            for z in range(planes):
                there = (z + by) % planes if e % CORES == 0 else (z - by) % planes
                pairs.append((e * planes + z, e * planes + there))
        return lax.ppermute(value, ("expert", "fsdp"), pairs)

    me = lax.axis_index("expert")
    plane = lax.axis_index("fsdp")
    core = me % CORES

    def relay(chunk):
        up_three = shift(chunk[3], 1)
        down_three = shift(chunk[-3], -1)
        four = shift_by_core(chunk[4], 2)
        up_one = shift(chunk[1], 1)
        down_one = shift(chunk[-1], -1)
        arrays = (chunk[2], up_three, chunk[-2], down_three, four)
        up_two, down_two = call(relay_kernel, [four.shape] * 2, [core], arrays)
        return chunk[0], up_one, down_one, shift(up_two, 2), shift(down_two, -2)

    def to_all_planes(value):
        next_two, last_two = shift(value, -2), shift(value, 2)
        next_one, last_one = shift(value, -1), shift(value, 1)
        four = shift_by_core(jnp.where(core == 0, next_two, last_two), -2)
        next_three, last_three = shift(next_two, -1), shift(last_two, 1)
        return value, next_one, next_two, next_three, four, last_three, last_two, last_one

    def gather_rows(slot_rows):
        mine = across(slot_rows.reshape(EXPERTS, -1, LANES), matching)
        mine = mine.reshape(1, EXPERTS * MOST, -1)
        near = across(jnp.broadcast_to(mine, (chips,) + mine.shape[1:]), same_core)
        near = near.reshape(half, -1)
        return near, swap(near)

    def give_back(near, far):
        [mine] = call(add_kernel, [near.shape], [], [near, swap(far)])
        arrived = across(mine.reshape(chips, EXPERTS * MOST, -1), same_core)
        [summed] = call(fold_kernel, [arrived.shape[1:]], [], [arrived])
        back = across(summed.reshape(EXPERTS, -1, LANES), matching)
        return back.reshape(EXPERTS * MOST, -1)

    bf16 = jnp.bfloat16
    def load(weights, earlier):
        return pl.pallas_call(
            load_kernel,
            out_shape=[pltpu.VMEM(w.shape, w.dtype) for w in weights],
            in_specs=[pl.BlockSpec(memory_space=pl.ANY)] * len(weights),
            out_specs=[VMEM] * len(weights),
            scratch_shapes=[pltpu.SemaphoreType.DMA((len(weights),))],
            compiler_params=PARAMS,
            cost_estimate=pl.CostEstimate(flops=0, bytes_accessed=4 << 20, transcendentals=0),
        )(*lax.optimization_barrier((*weights, earlier))[:-1])

    weights = [w_gate, w_up, w_down]
    [slots] = call(
        pack_kernel,
        [(EXPERTS * MOST, 2 * width)],
        [],
        [expert_ids, route_logits, tokens, out_grad],
    )
    near, far = gather_rows(slots)
    chunks = call(
        parts_kernel,
        [(own, 3 * hidden_width)] * planes,
        [plane],
        [near, far, *load(weights, near)],
        scratch=[pltpu.VMEM((rows, 3 * hidden_width), bf16)],
        flops=6 * rows * width * hidden_width,
    )
    arrived = jnp.concatenate([near[:, :width], far[:, :width]], axis=0)
    arrived_cot = jnp.concatenate([near[:, width:], far[:, width:]], axis=0)
    [value] = call(hidden_kernel, [(own, 3 * hidden_width + LANES)], [], relay(chunks))
    pieces = to_all_planes(value)
    near_part, far_part, hidden, gate_cot, up_cot = call(
        back_kernel,
        [(half, 2 * width + LANES)] * 2 + [(rows, hidden_width)] * 3,
        [plane],
        [*load(weights, pieces[2]), *pieces],
        scratch=[pltpu.VMEM((rows, LANES), bf16)],
        flops=6 * rows * width * hidden_width,
    )
    back = give_back(near_part, far_part)
    down_grad = contract(hidden, arrived_cot, 0, 0).astype(jnp.bfloat16)
    gate_grad = contract(arrived, gate_cot, 0, 0).astype(jnp.bfloat16)
    up_grad = contract(arrived, up_cot, 0, 0).astype(jnp.bfloat16)

    layer_out, tokens_grad, logits_grad = pl.pallas_call(
        combine_kernel,
        out_shape=[
            jax.ShapeDtypeStruct((count, width), bf16),
            jax.ShapeDtypeStruct((count, width), bf16),
            jax.ShapeDtypeStruct(route_logits.shape, jnp.float32),
        ],
        in_specs=[VMEM] * 3,
        out_specs=[VMEM] * 3,
        compiler_params=PARAMS,
    )(expert_ids, route_logits, back)
    return (layer_out, tokens_grad, gate_grad, up_grad, down_grad, logits_grad)


def solution(mesh):
    return jax.shard_map(
        on_device,
        mesh=mesh,
        in_specs=(
            P("expert", "fsdp"),
            P("expert", None),
            P("expert", None),
            P("fsdp", "expert"),
            P("fsdp", "expert"),
            P("expert", "fsdp"),
            P("expert", "fsdp"),
        ),
        out_specs=(
            P("expert", "fsdp"),
            P("expert", "fsdp"),
            P("fsdp", "expert"),
            P("fsdp", "expert"),
            P("expert", "fsdp"),
            P("expert", None),
        ),
        check_vma=False,
    )
```

```python
import jax
import jax.numpy as jnp
from jax import lax
from jax.experimental import pallas as pl
from jax.experimental.pallas import tpu as pltpu
from jax.sharding import PartitionSpec as P

EXPERTS = 4
MOST = 10
CORES = 2
LANES = 128


def contract(left, right, left_dim, right_dim):
    return lax.dot_general(
        left, right, (((left_dim,), (right_dim,)), ((), ())), preferred_element_type=jnp.float32
    )


VMEM = pl.BlockSpec(memory_space=pltpu.VMEM)
SMEM = pl.BlockSpec(memory_space=pltpu.SMEM)
PARAMS = pltpu.CompilerParams(vmem_limit_bytes=40 * 1024 * 1024)


def column(row):
    count = row.shape[1]
    down = lax.broadcasted_iota(jnp.int32, (count, count), 0)
    across = lax.broadcasted_iota(jnp.int32, (count, count), 1)
    return jnp.sum(jnp.where(down == across, row, 0.0), axis=1, keepdims=True)


def route_masks(ids_ref, logits_ref):
    count = ids_ref.shape[1]
    slots = EXPERTS * MOST
    slot = lax.broadcasted_iota(jnp.int32, (count, slots), 1)
    expert = jnp.zeros((count, slots), jnp.int32)
    for e in range(1, EXPERTS):
        expert = expert + (slot >= e * MOST).astype(jnp.int32)
    ids = [column(ids_ref[k : k + 1, :].astype(jnp.float32)) for k in range(2)]
    named = [i == expert.astype(jnp.float32) for i in ids]
    chosen = (named[0] | named[1]).astype(jnp.float32)
    row = lax.broadcasted_iota(jnp.int32, (count, count), 0)
    place = lax.broadcasted_iota(jnp.int32, (count, count), 1)
    before = (place < row).astype(jnp.float32)
    rank = jnp.dot(before, chosen, preferred_element_type=jnp.float32)
    placed = rank == (slot - expert * MOST).astype(jnp.float32)
    masks = [(n & placed).astype(jnp.bfloat16) for n in named]
    first = column(jax.nn.sigmoid(logits_ref[0:1, :] - logits_ref[1:2, :]))
    return masks, (first, 1.0 - first)


def pack_kernel(ids_ref, logits_ref, tokens_ref, grad_ref, slots_ref):
    width = tokens_ref.shape[1]
    masks, weights = route_masks(ids_ref, logits_ref)
    grad = grad_ref[...].astype(jnp.float32)
    cots = [(w * grad).astype(jnp.bfloat16) for w in weights]
    slots_ref[:, :width] = contract(masks[0] + masks[1], tokens_ref[...], 0, 0).astype(
        jnp.bfloat16
    )
    slots_ref[:, width:] = (
        contract(masks[0], cots[0], 0, 0) + contract(masks[1], cots[1], 0, 0)
    ).astype(jnp.bfloat16)


def load_kernel(*refs):
    count = len(refs) // 2
    copies = [
        pltpu.make_async_copy(refs[i], refs[count + i], refs[2 * count].at[i]) for i in range(count)
    ]
    for copy in copies:
        copy.start()
    for copy in copies:
        copy.wait()


def parts_kernel(plane_ref, near_ref, far_ref, gate_ref, up_ref, down_ref, *rest):
    chunks, parts_ref = rest[:-1], rest[-1]
    half = near_ref.shape[0]
    depth, units = gate_ref.shape
    own = chunks[0].shape[0]
    for start, rows_ref in ((0, near_ref), (half, far_ref)):
        rows = rows_ref[:, :depth]
        cots = rows_ref[:, depth:]
        at = slice(start, start + half)
        gate = jnp.dot(rows, gate_ref[...], preferred_element_type=jnp.float32)
        parts_ref[at, :units] = gate.astype(jnp.bfloat16)
        upper = jnp.dot(rows, up_ref[...], preferred_element_type=jnp.float32)
        parts_ref[at, units : 2 * units] = upper.astype(jnp.bfloat16)
        hidden_cot = contract(cots, down_ref[...], 1, 1)
        parts_ref[at, 2 * units :] = hidden_cot.astype(jnp.bfloat16)
    for ahead, chunk_ref in enumerate(chunks):
        at = lax.rem(plane_ref[0] + ahead, len(chunks)) * own
        chunk_ref[...] = parts_ref[pl.ds(pl.multiple_of(at, 16), own), :]


def product_block(product):
    near = product.astype(jnp.bfloat16).astype(jnp.float32)
    lane = lax.broadcasted_iota(jnp.int32, (product.shape[0], LANES), 1)
    block = jnp.where(lane == 0, near, jnp.where(lane == 1, product - near, 0.0))
    return block.astype(jnp.bfloat16)


def store_narrow(ref, summed):
    ref[:, :-LANES] = summed[:, :-LANES].astype(jnp.bfloat16)
    tail = summed[:, -LANES:]
    ref[:, -LANES:] = product_block(tail[:, 0:1] + tail[:, 1:2])


def relay_kernel(core_ref, up_ref, up_three_ref, down_ref, down_three_ref, four_ref, *outs):
    even = core_ref[0] == 0
    four = four_ref[...].astype(jnp.float32)
    up = up_ref[...].astype(jnp.float32) + up_three_ref[...].astype(jnp.float32)
    outs[0][...] = (up + jnp.where(even, four, 0.0)).astype(jnp.bfloat16)
    down = down_ref[...].astype(jnp.float32) + down_three_ref[...].astype(jnp.float32)
    outs[1][...] = (down + jnp.where(even, 0.0, four)).astype(jnp.bfloat16)


def hidden_kernel(a_ref, b_ref, c_ref, d_ref, e_ref, value_ref):
    units = a_ref.shape[1] // 3

    def summed(columns):
        total = a_ref[:, columns].astype(jnp.float32)
        for ref in (b_ref, c_ref, d_ref, e_ref):
            total = total + ref[:, columns].astype(jnp.float32)
        return total

    gate = summed(slice(0, units))
    upper = summed(slice(units, 2 * units))
    hidden_cot = summed(slice(2 * units, 3 * units))
    sig = jax.nn.sigmoid(gate)
    hidden = (gate * sig * upper).astype(jnp.bfloat16)
    value_ref[:, :units] = hidden
    gate_cot = hidden_cot * upper * sig * (1.0 + gate * (1.0 - sig))
    value_ref[:, units : 2 * units] = gate_cot.astype(jnp.bfloat16)
    value_ref[:, 2 * units : 3 * units] = (hidden_cot * gate * sig).astype(jnp.bfloat16)
    product = jnp.sum(hidden.astype(jnp.float32) * hidden_cot, axis=1, keepdims=True)
    value_ref[:, 3 * units :] = product_block(product)


def back_kernel(plane_ref, gate_ref, up_ref, down_ref, *rest):
    pieces, (near_ref, far_ref, hidden_ref, gate_cot_ref, up_cot_ref, tail_ref) = rest[:8], rest[8:]
    own = pieces[0].shape[0]
    half = near_ref.shape[0]
    depth, units = gate_ref.shape
    for ahead, piece in enumerate(pieces):
        at = pl.multiple_of(lax.rem(plane_ref[0] + ahead, len(pieces)) * own, 16)
        at = pl.ds(at, own)
        hidden_ref[at, :] = piece[:, :units]
        gate_cot_ref[at, :] = piece[:, units : 2 * units]
        up_cot_ref[at, :] = piece[:, 2 * units : 3 * units]
        tail_ref[at, :] = piece[:, 3 * units :]
    for start, ref in ((half, far_ref), (0, near_ref)):
        at = slice(start, start + half)
        out = jnp.dot(hidden_ref[at, :], down_ref[...], preferred_element_type=jnp.float32)
        ref[:, :depth] = out.astype(jnp.bfloat16)
        grad = contract(gate_cot_ref[at, :], gate_ref[...], 1, 1)
        grad = grad + contract(up_cot_ref[at, :], up_ref[...], 1, 1)
        ref[:, depth : 2 * depth] = grad.astype(jnp.bfloat16)
        ref[:, 2 * depth :] = tail_ref[at, :]


def add_kernel(near_ref, far_ref, sum_ref):
    store_narrow(sum_ref, near_ref[...].astype(jnp.float32) + far_ref[...].astype(jnp.float32))


def fold_kernel(blocks_ref, sum_ref):
    total = blocks_ref[0].astype(jnp.float32)
    for i in range(1, blocks_ref.shape[0]):
        total = total + blocks_ref[i].astype(jnp.float32)
    store_narrow(sum_ref, total)


def call(kernel, outs, scalars, arrays, scratch=(), flops=0):
    return pl.pallas_call(
        kernel,
        out_shape=[pltpu.VMEM(shape, jnp.bfloat16) for shape in outs],
        in_specs=[SMEM] * len(scalars) + [VMEM] * len(arrays),
        out_specs=[VMEM] * len(outs),
        scratch_shapes=scratch,
        compiler_params=PARAMS,
        cost_estimate=pl.CostEstimate(flops=flops, bytes_accessed=4 << 20, transcendentals=0),
    )(*[value.reshape(1) for value in scalars], *arrays)


def combine_kernel(ids_ref, logits_ref, back_ref, out_ref, tokens_ref, logits_grad_ref):
    width = out_ref.shape[1]
    masks, weights = route_masks(ids_ref, logits_ref)

    def pick(mask, columns):
        return jnp.dot(mask, back_ref[:, columns], preferred_element_type=jnp.float32)

    outs = [pick(m, slice(0, width)) for m in masks]
    out_ref[...] = (weights[0] * outs[0] + weights[1] * outs[1]).astype(jnp.bfloat16)
    tokens_ref[...] = pick(masks[0] + masks[1], slice(width, 2 * width)).astype(jnp.bfloat16)
    products = [pick(m, slice(2 * width, 2 * width + LANES)) for m in masks]
    products = [p[:, 0:1] + p[:, 1:2] for p in products]
    change = products[0] * weights[1] - products[1] * weights[0]
    count = change.shape[0]
    down = lax.broadcasted_iota(jnp.int32, (count, count), 0)
    across = lax.broadcasted_iota(jnp.int32, (count, count), 1)
    change = jnp.sum(jnp.where(down == across, change, 0.0), axis=0, keepdims=True)
    logits_grad_ref[0:1, :] = change
    logits_grad_ref[1:2, :] = -change


def on_device(tokens, expert_ids, route_logits, w_gate, w_up, w_down, out_grad):
    count, width = tokens.shape
    hidden_width = w_gate.shape[1]
    peers = lax.axis_size("expert")
    planes = lax.axis_size("fsdp")
    group = peers // EXPERTS
    chips = group // CORES
    half = peers // CORES * MOST
    rows = CORES * half
    own = rows // planes
    matching = [[group * e + i for e in range(EXPERTS)] for i in range(group)]
    same_core = [
        [group * e + CORES * p + c for p in range(chips)]
        for e in range(EXPERTS)
        for c in range(CORES)
    ]
    other_core = [(i, i ^ 1) for i in range(peers)]

    def across(blocks, groups):
        return lax.all_to_all(
            blocks, "expert", split_axis=0, concat_axis=0, axis_index_groups=groups, tiled=True
        )

    def swap(value):
        return lax.ppermute(value, "expert", other_core)

    def shift(value, by):
        pairs = [(i, (i + by) % planes) for i in range(planes)]
        return lax.ppermute(value, "fsdp", pairs)

    def shift_by_core(value, by):
        pairs = []
        for e in range(peers):
            for z in range(planes):
                there = (z + by) % planes if e % CORES == 0 else (z - by) % planes
                pairs.append((e * planes + z, e * planes + there))
        return lax.ppermute(value, ("expert", "fsdp"), pairs)

    me = lax.axis_index("expert")
    plane = lax.axis_index("fsdp")
    core = me % CORES

    def relay(chunk):
        up_three = shift(chunk[3], 1)
        down_three = shift(chunk[-3], -1)
        four = shift_by_core(chunk[4], 2)
        up_one = shift(chunk[1], 1)
        down_one = shift(chunk[-1], -1)
        arrays = (chunk[2], up_three, chunk[-2], down_three, four)
        up_two, down_two = call(relay_kernel, [four.shape] * 2, [core], arrays)
        return chunk[0], up_one, down_one, shift(up_two, 2), shift(down_two, -2)

    def to_all_planes(value):
        next_two, last_two = shift(value, -2), shift(value, 2)
        next_one, last_one = shift(value, -1), shift(value, 1)
        four = shift_by_core(jnp.where(core == 0, next_two, last_two), -2)
        next_three, last_three = shift(next_two, -1), shift(last_two, 1)
        return value, next_one, next_two, next_three, four, last_three, last_two, last_one

    def gather_rows(slot_rows):
        mine = across(slot_rows.reshape(EXPERTS, -1, LANES), matching)
        mine = mine.reshape(1, EXPERTS * MOST, -1)
        near = across(jnp.broadcast_to(mine, (chips,) + mine.shape[1:]), same_core)
        near = near.reshape(half, -1)
        return near, swap(near)

    def give_back(near, far):
        [mine] = call(add_kernel, [near.shape], [], [near, swap(far)])
        arrived = across(mine.reshape(chips, EXPERTS * MOST, -1), same_core)
        [summed] = call(fold_kernel, [arrived.shape[1:]], [], [arrived])
        back = across(summed.reshape(EXPERTS, -1, LANES), matching)
        return back.reshape(EXPERTS * MOST, -1)

    bf16 = jnp.bfloat16
    def load(weights, earlier):
        return pl.pallas_call(
            load_kernel,
            out_shape=[pltpu.VMEM(w.shape, w.dtype) for w in weights],
            in_specs=[pl.BlockSpec(memory_space=pl.ANY)] * len(weights),
            out_specs=[VMEM] * len(weights),
            scratch_shapes=[pltpu.SemaphoreType.DMA((len(weights),))],
            compiler_params=PARAMS,
            cost_estimate=pl.CostEstimate(flops=0, bytes_accessed=4 << 20, transcendentals=0),
        )(*lax.optimization_barrier((*weights, earlier))[:-1])

    weights = [w_gate, w_up, w_down]
    small = [expert_ids.T, route_logits.T]
    [slots] = call(
        pack_kernel,
        [(EXPERTS * MOST, 2 * width)],
        [],
        [*small, tokens, out_grad],
    )
    near, far = gather_rows(slots)
    chunks = call(
        parts_kernel,
        [(own, 3 * hidden_width)] * planes,
        [plane],
        [near, far, *load(weights, near)],
        scratch=[pltpu.VMEM((rows, 3 * hidden_width), bf16)],
        flops=6 * rows * width * hidden_width,
    )
    arrived = jnp.concatenate([near[:, :width], far[:, :width]], axis=0)
    arrived_cot = jnp.concatenate([near[:, width:], far[:, width:]], axis=0)
    [value] = call(hidden_kernel, [(own, 3 * hidden_width + LANES)], [], relay(chunks))
    pieces = to_all_planes(value)
    near_part, far_part, hidden, gate_cot, up_cot = call(
        back_kernel,
        [(half, 2 * width + LANES)] * 2 + [(rows, hidden_width)] * 3,
        [plane],
        [*load(weights, pieces[2]), *pieces],
        scratch=[pltpu.VMEM((rows, LANES), bf16)],
        flops=6 * rows * width * hidden_width,
    )
    back = give_back(near_part, far_part)
    down_grad = contract(hidden, arrived_cot, 0, 0).astype(jnp.bfloat16)
    gate_grad = contract(arrived, gate_cot, 0, 0).astype(jnp.bfloat16)
    up_grad = contract(arrived, up_cot, 0, 0).astype(jnp.bfloat16)

    layer_out, tokens_grad, logits_grad = pl.pallas_call(
        combine_kernel,
        out_shape=[
            jax.ShapeDtypeStruct((count, width), bf16),
            jax.ShapeDtypeStruct((count, width), bf16),
            jax.ShapeDtypeStruct(small[1].shape, jnp.float32),
        ],
        in_specs=[VMEM] * 3,
        out_specs=[VMEM] * 3,
        compiler_params=PARAMS,
    )(*small, back)
    return (layer_out, tokens_grad, gate_grad, up_grad, down_grad, logits_grad.T)


def solution(mesh):
    return jax.shard_map(
        on_device,
        mesh=mesh,
        in_specs=(
            P("expert", "fsdp"),
            P("expert", None),
            P("expert", None),
            P("fsdp", "expert"),
            P("fsdp", "expert"),
            P("expert", "fsdp"),
            P("expert", "fsdp"),
        ),
        out_specs=(
            P("expert", "fsdp"),
            P("expert", "fsdp"),
            P("fsdp", "expert"),
            P("fsdp", "expert"),
            P("expert", "fsdp"),
            P("expert", None),
        ),
        check_vma=False,
    )
```

```python
import jax
import jax.numpy as jnp
from jax import lax
from jax.experimental import pallas as pl
from jax.experimental.pallas import tpu as pltpu
from jax.sharding import PartitionSpec as P

EXPERTS = 4
MOST = 10
CORES = 2
LANES = 128


def contract(left, right, left_dim, right_dim):
    return lax.dot_general(
        left, right, (((left_dim,), (right_dim,)), ((), ())), preferred_element_type=jnp.float32
    )


VMEM = pl.BlockSpec(memory_space=pltpu.VMEM)
SMEM = pl.BlockSpec(memory_space=pltpu.SMEM)
PARAMS = pltpu.CompilerParams(vmem_limit_bytes=40 * 1024 * 1024)


def column(row):
    count = row.shape[1]
    down = lax.broadcasted_iota(jnp.int32, (count, count), 0)
    across = lax.broadcasted_iota(jnp.int32, (count, count), 1)
    return jnp.sum(jnp.where(down == across, row, 0.0), axis=1, keepdims=True)


def route_masks(ids_ref, logits_ref):
    count = ids_ref.shape[1]
    slots = EXPERTS * MOST
    slot = lax.broadcasted_iota(jnp.int32, (count, slots), 1)
    expert = jnp.zeros((count, slots), jnp.int32)
    for e in range(1, EXPERTS):
        expert = expert + (slot >= e * MOST).astype(jnp.int32)
    ids = [column(ids_ref[k : k + 1, :].astype(jnp.float32)) for k in range(2)]
    named = [i == expert.astype(jnp.float32) for i in ids]
    chosen = (named[0] | named[1]).astype(jnp.float32)
    row = lax.broadcasted_iota(jnp.int32, (count, count), 0)
    place = lax.broadcasted_iota(jnp.int32, (count, count), 1)
    before = (place < row).astype(jnp.float32)
    rank = jnp.dot(before, chosen, preferred_element_type=jnp.float32)
    placed = rank == (slot - expert * MOST).astype(jnp.float32)
    masks = [(n & placed).astype(jnp.bfloat16) for n in named]
    first = column(jax.nn.sigmoid(logits_ref[0:1, :] - logits_ref[1:2, :]))
    return masks, (first, 1.0 - first)


def pack_kernel(ids_ref, logits_ref, tokens_ref, grad_ref, slots_ref):
    width = tokens_ref.shape[1]
    masks, weights = route_masks(ids_ref, logits_ref)
    grad = grad_ref[...].astype(jnp.float32)
    cots = [(w * grad).astype(jnp.bfloat16) for w in weights]
    slots_ref[:, :width] = contract(masks[0] + masks[1], tokens_ref[...], 0, 0).astype(
        jnp.bfloat16
    )
    slots_ref[:, width:] = (
        contract(masks[0], cots[0], 0, 0) + contract(masks[1], cots[1], 0, 0)
    ).astype(jnp.bfloat16)


def load_kernel(*refs):
    count = len(refs) // 2
    copies = [
        pltpu.make_async_copy(refs[i], refs[count + i], refs[2 * count].at[i]) for i in range(count)
    ]
    for copy in copies:
        copy.start()
    for copy in copies:
        copy.wait()


def parts_kernel(plane_ref, near_ref, far_ref, gate_ref, up_ref, down_ref, *rest):
    chunks, parts_ref = rest[:-1], rest[-1]
    half = near_ref.shape[0]
    depth, units = gate_ref.shape
    own = chunks[0].shape[0]
    for start, rows_ref in ((0, near_ref), (half, far_ref)):
        rows = rows_ref[:, :depth]
        cots = rows_ref[:, depth:]
        at = slice(start, start + half)
        gate = jnp.dot(rows, gate_ref[...], preferred_element_type=jnp.float32)
        parts_ref[at, :units] = gate.astype(jnp.bfloat16)
        upper = jnp.dot(rows, up_ref[...], preferred_element_type=jnp.float32)
        parts_ref[at, units : 2 * units] = upper.astype(jnp.bfloat16)
        hidden_cot = contract(cots, down_ref[...], 1, 1)
        parts_ref[at, 2 * units :] = hidden_cot.astype(jnp.bfloat16)
    for ahead, chunk_ref in enumerate(chunks):
        at = lax.rem(plane_ref[0] + ahead, len(chunks)) * own
        chunk_ref[...] = parts_ref[pl.ds(pl.multiple_of(at, 16), own), :]


def product_block(product):
    near = product.astype(jnp.bfloat16).astype(jnp.float32)
    lane = lax.broadcasted_iota(jnp.int32, (product.shape[0], LANES), 1)
    block = jnp.where(lane == 0, near, jnp.where(lane == 1, product - near, 0.0))
    return block.astype(jnp.bfloat16)


def store_narrow(ref, summed):
    ref[:, :-LANES] = summed[:, :-LANES].astype(jnp.bfloat16)
    tail = summed[:, -LANES:]
    ref[:, -LANES:] = product_block(tail[:, 0:1] + tail[:, 1:2])


def relay_kernel(core_ref, up_ref, up_three_ref, down_ref, down_three_ref, four_ref, *outs):
    even = core_ref[0] == 0
    four = four_ref[...].astype(jnp.float32)
    up = up_ref[...].astype(jnp.float32) + up_three_ref[...].astype(jnp.float32)
    outs[0][...] = (up + jnp.where(even, four, 0.0)).astype(jnp.bfloat16)
    down = down_ref[...].astype(jnp.float32) + down_three_ref[...].astype(jnp.float32)
    outs[1][...] = (down + jnp.where(even, 0.0, four)).astype(jnp.bfloat16)


def hidden_kernel(a_ref, b_ref, c_ref, d_ref, e_ref, value_ref):
    units = a_ref.shape[1] // 3

    def summed(columns):
        total = a_ref[:, columns].astype(jnp.float32)
        for ref in (b_ref, c_ref, d_ref, e_ref):
            total = total + ref[:, columns].astype(jnp.float32)
        return total

    gate = summed(slice(0, units))
    upper = summed(slice(units, 2 * units))
    hidden_cot = summed(slice(2 * units, 3 * units))
    sig = jax.nn.sigmoid(gate)
    hidden = (gate * sig * upper).astype(jnp.bfloat16)
    value_ref[:, :units] = hidden
    gate_cot = hidden_cot * upper * sig * (1.0 + gate * (1.0 - sig))
    value_ref[:, units : 2 * units] = gate_cot.astype(jnp.bfloat16)
    value_ref[:, 2 * units : 3 * units] = (hidden_cot * gate * sig).astype(jnp.bfloat16)
    product = jnp.sum(hidden.astype(jnp.float32) * hidden_cot, axis=1, keepdims=True)
    value_ref[:, 3 * units :] = product_block(product)


def back_half(start, gate_ref, up_ref, down_ref, hidden_ref, gate_cot_ref, up_cot_ref, tail_ref, ref):
    half = ref.shape[0]
    depth = gate_ref.shape[0]
    at = slice(start, start + half)
    out = jnp.dot(hidden_ref[at, :], down_ref[...], preferred_element_type=jnp.float32)
    ref[:, :depth] = out.astype(jnp.bfloat16)
    grad = contract(gate_cot_ref[at, :], gate_ref[...], 1, 1)
    grad = grad + contract(up_cot_ref[at, :], up_ref[...], 1, 1)
    ref[:, depth : 2 * depth] = grad.astype(jnp.bfloat16)
    ref[:, 2 * depth :] = tail_ref[at, :]


def far_kernel(plane_ref, gate_ref, up_ref, down_ref, *rest):
    pieces, (far_ref, *whole) = rest[:8], rest[8:]
    own = pieces[0].shape[0]
    units = whole[0].shape[1]
    for ahead, piece in enumerate(pieces):
        at = pl.multiple_of(lax.rem(plane_ref[0] + ahead, len(pieces)) * own, 16)
        for i, ref in enumerate(whole):
            ref[pl.ds(at, own), :] = piece[:, i * units : i * units + ref.shape[1]]
    back_half(far_ref.shape[0], gate_ref, up_ref, down_ref, *whole, far_ref)


def near_kernel(*refs):
    back_half(0, *refs)


def add_kernel(near_ref, far_ref, sum_ref):
    store_narrow(sum_ref, near_ref[...].astype(jnp.float32) + far_ref[...].astype(jnp.float32))


def fold_kernel(blocks_ref, sum_ref):
    total = blocks_ref[0].astype(jnp.float32)
    for i in range(1, blocks_ref.shape[0]):
        total = total + blocks_ref[i].astype(jnp.float32)
    store_narrow(sum_ref, total)


def call(kernel, outs, scalars, arrays, scratch=(), flops=0):
    return pl.pallas_call(
        kernel,
        out_shape=[pltpu.VMEM(shape, jnp.bfloat16) for shape in outs],
        in_specs=[SMEM] * len(scalars) + [VMEM] * len(arrays),
        out_specs=[VMEM] * len(outs),
        scratch_shapes=scratch,
        compiler_params=PARAMS,
        cost_estimate=pl.CostEstimate(flops=flops, bytes_accessed=4 << 20, transcendentals=0),
    )(*[value.reshape(1) for value in scalars], *arrays)


def combine_kernel(ids_ref, logits_ref, back_ref, out_ref, tokens_ref, logits_grad_ref):
    width = out_ref.shape[1]
    masks, weights = route_masks(ids_ref, logits_ref)

    def pick(mask, columns):
        return jnp.dot(mask, back_ref[:, columns], preferred_element_type=jnp.float32)

    outs = [pick(m, slice(0, width)) for m in masks]
    out_ref[...] = (weights[0] * outs[0] + weights[1] * outs[1]).astype(jnp.bfloat16)
    tokens_ref[...] = pick(masks[0] + masks[1], slice(width, 2 * width)).astype(jnp.bfloat16)
    products = [pick(m, slice(2 * width, 2 * width + LANES)) for m in masks]
    products = [p[:, 0:1] + p[:, 1:2] for p in products]
    change = products[0] * weights[1] - products[1] * weights[0]
    count = change.shape[0]
    down = lax.broadcasted_iota(jnp.int32, (count, count), 0)
    across = lax.broadcasted_iota(jnp.int32, (count, count), 1)
    change = jnp.sum(jnp.where(down == across, change, 0.0), axis=0, keepdims=True)
    logits_grad_ref[0:1, :] = change
    logits_grad_ref[1:2, :] = -change


def on_device(tokens, expert_ids, route_logits, w_gate, w_up, w_down, out_grad):
    count, width = tokens.shape
    hidden_width = w_gate.shape[1]
    peers = lax.axis_size("expert")
    planes = lax.axis_size("fsdp")
    group = peers // EXPERTS
    chips = group // CORES
    half = peers // CORES * MOST
    rows = CORES * half
    own = rows // planes
    matching = [[group * e + i for e in range(EXPERTS)] for i in range(group)]
    same_core = [
        [group * e + CORES * p + c for p in range(chips)]
        for e in range(EXPERTS)
        for c in range(CORES)
    ]
    other_core = [(i, i ^ 1) for i in range(peers)]

    def across(blocks, groups):
        return lax.all_to_all(
            blocks, "expert", split_axis=0, concat_axis=0, axis_index_groups=groups, tiled=True
        )

    def swap(value):
        return lax.ppermute(value, "expert", other_core)

    def shift(value, by):
        pairs = [(i, (i + by) % planes) for i in range(planes)]
        return lax.ppermute(value, "fsdp", pairs)

    def shift_by_core(value, by):
        pairs = []
        for e in range(peers):
            for z in range(planes):
                there = (z + by) % planes if e % CORES == 0 else (z - by) % planes
                pairs.append((e * planes + z, e * planes + there))
        return lax.ppermute(value, ("expert", "fsdp"), pairs)

    me = lax.axis_index("expert")
    plane = lax.axis_index("fsdp")
    core = me % CORES

    def relay(chunk):
        up_three = shift(chunk[3], 1)
        down_three = shift(chunk[-3], -1)
        four = shift_by_core(chunk[4], 2)
        up_one = shift(chunk[1], 1)
        down_one = shift(chunk[-1], -1)
        arrays = (chunk[2], up_three, chunk[-2], down_three, four)
        up_two, down_two = call(relay_kernel, [four.shape] * 2, [core], arrays)
        return chunk[0], up_one, down_one, shift(up_two, 2), shift(down_two, -2)

    def to_all_planes(value):
        next_two, last_two = shift(value, -2), shift(value, 2)
        next_one, last_one = shift(value, -1), shift(value, 1)
        four = shift_by_core(jnp.where(core == 0, next_two, last_two), -2)
        next_three, last_three = shift(next_two, -1), shift(last_two, 1)
        return value, next_one, next_two, next_three, four, last_three, last_two, last_one

    def gather_rows(slot_rows):
        mine = across(slot_rows.reshape(EXPERTS, -1, LANES), matching)
        mine = mine.reshape(1, EXPERTS * MOST, -1)
        near = across(jnp.broadcast_to(mine, (chips,) + mine.shape[1:]), same_core)
        near = near.reshape(half, -1)
        return near, swap(near)

    def give_back(near, swapped):
        [mine] = call(add_kernel, [near.shape], [], [near, swapped])
        arrived = across(mine.reshape(chips, EXPERTS * MOST, -1), same_core)
        [summed] = call(fold_kernel, [arrived.shape[1:]], [], [arrived])
        back = across(summed.reshape(EXPERTS, -1, LANES), matching)
        return back.reshape(EXPERTS * MOST, -1)

    bf16 = jnp.bfloat16
    def load(weights, earlier):
        return pl.pallas_call(
            load_kernel,
            out_shape=[pltpu.VMEM(w.shape, w.dtype) for w in weights],
            in_specs=[pl.BlockSpec(memory_space=pl.ANY)] * len(weights),
            out_specs=[VMEM] * len(weights),
            scratch_shapes=[pltpu.SemaphoreType.DMA((len(weights),))],
            compiler_params=PARAMS,
            cost_estimate=pl.CostEstimate(flops=0, bytes_accessed=4 << 20, transcendentals=0),
        )(*lax.optimization_barrier((*weights, earlier))[:-1])

    weights = [w_gate, w_up, w_down]
    small = [expert_ids.T, route_logits.T]
    [slots] = call(
        pack_kernel,
        [(EXPERTS * MOST, 2 * width)],
        [],
        [*small, tokens, out_grad],
    )
    near, far = gather_rows(slots)
    chunks = call(
        parts_kernel,
        [(own, 3 * hidden_width)] * planes,
        [plane],
        [near, far, *load(weights, near)],
        scratch=[pltpu.VMEM((rows, 3 * hidden_width), bf16)],
        flops=6 * rows * width * hidden_width,
    )
    arrived = jnp.concatenate([near[:, :width], far[:, :width]], axis=0)
    arrived_cot = jnp.concatenate([near[:, width:], far[:, width:]], axis=0)
    [value] = call(hidden_kernel, [(own, 3 * hidden_width + LANES)], [], relay(chunks))
    pieces = to_all_planes(value)
    held = load(weights, pieces[2])
    back_shape = (half, 2 * width + LANES)
    flops = 3 * rows * width * hidden_width
    far_part, hidden, gate_cot, up_cot, tail = call(
        far_kernel,
        [back_shape] + [(rows, hidden_width)] * 3 + [(rows, LANES)],
        [plane],
        [*held, *pieces],
        flops=flops,
    )
    swapped = swap(far_part)
    [near_part] = call(
        near_kernel, [back_shape], [], [*held, hidden, gate_cot, up_cot, tail], flops=flops
    )
    back = give_back(near_part, swapped)
    down_grad = contract(hidden, arrived_cot, 0, 0).astype(jnp.bfloat16)
    gate_grad = contract(arrived, gate_cot, 0, 0).astype(jnp.bfloat16)
    up_grad = contract(arrived, up_cot, 0, 0).astype(jnp.bfloat16)

    layer_out, tokens_grad, logits_grad = pl.pallas_call(
        combine_kernel,
        out_shape=[
            jax.ShapeDtypeStruct((count, width), bf16),
            jax.ShapeDtypeStruct((count, width), bf16),
            jax.ShapeDtypeStruct(small[1].shape, jnp.float32),
        ],
        in_specs=[VMEM] * 3,
        out_specs=[VMEM] * 3,
        compiler_params=PARAMS,
    )(*small, back)
    return (layer_out, tokens_grad, gate_grad, up_grad, down_grad, logits_grad.T)


def solution(mesh):
    return jax.shard_map(
        on_device,
        mesh=mesh,
        in_specs=(
            P("expert", "fsdp"),
            P("expert", None),
            P("expert", None),
            P("fsdp", "expert"),
            P("fsdp", "expert"),
            P("expert", "fsdp"),
            P("expert", "fsdp"),
        ),
        out_specs=(
            P("expert", "fsdp"),
            P("expert", "fsdp"),
            P("fsdp", "expert"),
            P("fsdp", "expert"),
            P("expert", "fsdp"),
            P("expert", None),
        ),
        check_vma=False,
    )
```
